32 devices in a mesh: section: 4 (over z), dp: 8 (over y, x, core).
Axes of the slice: x: 2, y: 2, z: 4, core: 2. Of those that a mesh axis runs over, the one named last changes fastest.
Arguments:
- block_input: bfloat16 [4, 8, 8, 64, 768], P('section', 'dp'), may hold values from -6 to 6
- grad_output: bfloat16 [4, 8, 8, 64, 768], P('section', 'dp'), may hold values from -6 to 6
- depth_weight: bfloat16 [4, 49, 768], P('section'), may hold values from -0.875 to 0.875
- depth_bias: float32 [4, 768], P('section'), may hold values from -0.5 to 0.5
- norm_gain: float32 [4, 768], P('section'), may hold values from 0.25 to 1.75
- norm_shift: float32 [4, 768], P('section'), may hold values from -0.5 to 0.5
- pw1_weight: bfloat16 [4, 3072, 768], P('section'), may hold values from -0.21875 to 0.21875
- pw1_bias: float32 [4, 3072], P('section'), may hold values from -1 to 1
- pw2_weight: bfloat16 [4, 768, 3072], P('section'), may hold values from -0.109375 to 0.109375
- pw2_bias: float32 [4, 768], P('section'), may hold values from -0.5 to 0.5
- layer_scale: float32 [4, 768], P('section'), may hold values from 0.2 to 2
Outputs:
- grad_pw1: float32 [4, 3072, 768], P('section', 'dp')
- grad_pw2: float32 [4, 768, 3072], P('section', None, 'dp')
- grad_bias1: float32 [4, 3072], P('section')
- grad_small: float32 [4, 54, 768], P('section')
- received: bfloat16 [4, 8, 8, 64, 768], P('section', 'dp')
The draws below stay inside these ranges and needn't reach their ends.
All inputs are finite; a program needn't handle non-finite values.
Results may differ from the reference program's by a relative error of at most 0.0061.
Values may be sent and summed in bfloat16 or wider, within the bound.
No kernel may reach another device: no remote copies, remote signals or barrier semaphores. Data moves between devices by JAX's collectives and lax.ppermute only.
A program may use at most 256 MiB of HBM per device.

```python
import math
import jax
import jax.numpy as jnp
from jax import lax

C = 768
FF = 3072
WIN_H = 8
WIN_W = 64
REPLICAS = 8
SECTIONS = 4
N_DP = 8


def block_levels(key, shape, cuts, low, top_value):
    factor_of = 1.0
    for axis_at, blocks in cuts:
        heights = jax.random.uniform(jax.random.fold_in(jax.random.fold_in(key, 6), axis_at), (blocks,), jnp.float32, low / len(cuts), top_value / len(cuts))
        factor_of = factor_of * jnp.repeat(jnp.exp(heights), shape[axis_at] // blocks).reshape((-1,) + (1,) * (len(shape) - 1 - axis_at))
    return factor_of


def normal_values(rng, shape, width, reach, split=(), dtype=jnp.bfloat16):
    drawn = jax.random.normal(rng, shape, jnp.float32) * width
    if len(split) > 0:
        drawn = block_levels(rng, shape, split, -0.22, 0.18) * drawn
    return jnp.clip(drawn, min=-reach, max=reach).astype(dtype)


def setup_inputs(seed: int = 0) -> dict:
    seeds = jax.random.split(jax.random.key(seed), 12)
    return {
        "block_input": normal_values(seeds[0], (SECTIONS, REPLICAS, WIN_H, WIN_W, C), 1.0, 6.0, ((0, 4), (1, 8))),
        "grad_output": normal_values(seeds[1], (SECTIONS, REPLICAS, WIN_H, WIN_W, C), 1.0, 6.0, ((0, 4), (1, 8))),
        "depth_weight": normal_values(seeds[2], (SECTIONS, 49, C), 49 ** -0.5, 0.875, ((0, 4),)),
        "depth_bias": jnp.clip(jax.random.uniform(seeds[3], (SECTIONS, C), jnp.float32, -0.5, 0.5) * block_levels(seeds[3], (SECTIONS, C), ((0, 4),), -0.4, 0.0), -0.5, 0.5),
        "norm_gain": jnp.clip(1.0 + 0.15 * jax.random.normal(seeds[4], (SECTIONS, C), jnp.float32), 0.25, 1.75),
        "norm_shift": jnp.clip(jax.random.uniform(seeds[5], (SECTIONS, C), jnp.float32, -0.5, 0.5) * block_levels(seeds[5], (SECTIONS, C), ((0, 4),), -0.4, 0.0), -0.5, 0.5),
        "pw1_weight": normal_values(seeds[6], (SECTIONS, FF, C), C ** -0.5, 0.21875, ((0, 4),)),
        "pw1_bias": jnp.clip(jax.random.uniform(seeds[7], (SECTIONS, FF), jnp.float32, -1.0, 1.0) * block_levels(seeds[7], (SECTIONS, FF), ((0, 4),), -0.4, 0.0), -1.0, 1.0),
        "pw2_weight": normal_values(seeds[8], (SECTIONS, C, FF), FF ** -0.5, 0.109375, ((0, 4),)),
        "pw2_bias": jnp.clip(jax.random.uniform(seeds[9], (SECTIONS, C), jnp.float32, -0.5, 0.5) * block_levels(seeds[9], (SECTIONS, C), ((0, 4),), -0.4, 0.0), -0.5, 0.5),
        "layer_scale": jnp.clip(jnp.exp(math.log(2.0) - 2.3025851 * jax.random.uniform(seeds[10], (SECTIONS, C), jnp.float32) ** block_levels(seeds[10], (SECTIONS, C), ((0, 4),), -0.2, 0.2)), 0.2, 2.0),
    }


root_half = 0.7071067811865476
inv_root_two_pi = 0.3989422804014327

def contract_last(left, right):
    return lax.dot_general(left, right, (((1,), (1,)), ((), ())), preferred_element_type=jnp.float32)

def contract_first(left, right):
    return lax.dot_general(left, right, (((0,), (0,)), ((), ())), preferred_element_type=jnp.float32)

def tap_apply(padded, weights, rows, cols, flip):
    total = jnp.zeros((rows, cols, weights.shape[1]), jnp.float32)
    for i in range(7):
        for j in range(7):
            if flip:
                window = padded[6 - i:6 - i + rows, 6 - j:6 - j + cols]
            else:
                window = padded[i:i + rows, j:j + cols]
            total = total + window * weights[7 * i + j]
    return total

def tap_grads(padded, grad, rows, cols):
    pieces = []
    for i in range(7):
        for j in range(7):
            pieces.append(lax.optimization_barrier(jnp.sum(grad * padded[i:i + rows, j:j + cols], axis=(0, 1))))
    return jnp.stack(pieces)

def block_backward(block_x, block_g, depth_w, depth_b, gain, shift_b, w_one, b_one, w_two, b_two, scale):
    rows, cols, chans = block_x.shape
    cells = rows * cols
    inputs = block_x.astype(jnp.float32)
    padded = jnp.pad(inputs, ((3, 3), (3, 3), (0, 0)))
    weights = depth_w.astype(jnp.float32)
    depthwise = tap_apply(padded, weights, rows, cols, False) + depth_b
    centered = depthwise - lax.optimization_barrier(jnp.mean(depthwise, axis=-1, keepdims=True))
    rstd = lax.rsqrt(lax.optimization_barrier(jnp.mean(centered * centered, axis=-1, keepdims=True)) + 1e-06)
    normed = (centered * rstd).reshape(cells, chans)
    ynorm = (normed * gain + shift_b).astype(jnp.bfloat16)
    preact = contract_last(ynorm, w_one) + b_one
    cdf = 0.5 * (1.0 + lax.erf(preact * root_half))
    hidden = (preact * cdf).astype(jnp.bfloat16)
    branch = contract_last(hidden, w_two) + b_two
    grads = block_g.reshape(cells, chans).astype(jnp.float32)
    gscale_term = lax.optimization_barrier(jnp.sum(grads * branch, axis=0))
    gproj = (grads * scale).astype(jnp.bfloat16)
    b2_term = lax.optimization_barrier(jnp.sum(gproj.astype(jnp.float32), axis=0))
    w2_term = contract_first(gproj, hidden)
    ghidden = jnp.dot(gproj, w_two, preferred_element_type=jnp.float32)
    density = jnp.exp(-0.5 * preact * preact) * inv_root_two_pi
    gpre = (ghidden * (cdf + preact * density)).astype(jnp.bfloat16)
    b1_term = lax.optimization_barrier(jnp.sum(gpre.astype(jnp.float32), axis=0))
    w1_term = contract_first(gpre, ynorm)
    gnorm = jnp.dot(gpre, w_one, preferred_element_type=jnp.float32)
    gain_term = lax.optimization_barrier(jnp.sum(gnorm * normed, axis=0))
    shift_term = lax.optimization_barrier(jnp.sum(gnorm, axis=0))
    scaled_g = gnorm * gain
    gdepth = rstd.reshape(cells, 1) * (scaled_g - lax.optimization_barrier(jnp.mean(scaled_g, axis=-1, keepdims=True)) - normed * lax.optimization_barrier(jnp.mean(scaled_g * normed, axis=-1, keepdims=True)))
    gdepth = gdepth.reshape(rows, cols, chans)
    tap_term = tap_grads(padded, gdepth, rows, cols)
    dbias_term = lax.optimization_barrier(jnp.sum(gdepth, axis=(0, 1)))
    gpadded = jnp.pad(gdepth, ((3, 3), (3, 3), (0, 0)))
    ginput = (block_g.astype(jnp.float32) + tap_apply(gpadded, weights, rows, cols, True)).astype(jnp.bfloat16)
    small = jnp.concatenate([tap_term, jnp.stack([dbias_term, gain_term, shift_term, b2_term, gscale_term])], axis=0)
    return (ginput, w1_term, w2_term, b1_term, small)

def reference(block_input, grad_output, depth_weight, depth_bias, norm_gain, norm_shift, pw1_weight, pw1_bias, pw2_weight, pw2_bias, layer_scale):

    def per_section(packed):
        xs, gs, depth_w, depth_b, gain, shift_b, w_one, b_one, w_two, b_two, scale = packed
        chans = xs.shape[-1]
        hidden_n = w_one.shape[0]
        init = (jnp.zeros((hidden_n, chans), jnp.float32), jnp.zeros((chans, hidden_n), jnp.float32), jnp.zeros((hidden_n,), jnp.float32), jnp.zeros((54, chans), jnp.float32))

        def step(carry, pair):
            ginput, w1_term, w2_term, b1_term, small = block_backward(pair[0], pair[1], depth_w, depth_b, gain, shift_b, w_one, b_one, w_two, b_two, scale)
            return ((carry[0] + w1_term, carry[1] + w2_term, carry[2] + b1_term, carry[3] + small), ginput)
        sums, ginputs = lax.scan(step, init, (xs, gs))
        return (sums[0], sums[1], sums[2], sums[3], ginputs)
    w1_all, w2_all, b1_all, small_all, ginput_all = lax.map(per_section, (block_input, grad_output, depth_weight, depth_bias, norm_gain, norm_shift, pw1_weight, pw1_bias, pw2_weight, pw2_bias, layer_scale))
    factor = 1.0 / N_DP
    received = jnp.concatenate([ginput_all[1:], jnp.zeros_like(ginput_all[:1])], axis=0)
    return (w1_all * factor, w2_all * factor, b1_all * factor, small_all * factor, received)
```

```python
import jax
import jax.numpy as jnp
from jax import lax
from jax.experimental import pallas as pl
from jax.experimental.pallas import tpu as pltpu
from jax.sharding import PartitionSpec as P

root_half = 0.7071067811865476
inv_root_two_pi = 0.3989422804014327
f32 = jnp.float32
bf16 = jnp.bfloat16
LANES = 128
EDGE = 8
VMEM_LIMIT = 48 * 1024 * 1024


def struct(shape, dtype):
    return jax.ShapeDtypeStruct(shape, dtype)


def call(body, out_shape, *args, name, aliases=None, scratch=(), scalars=0, in_specs=None, cost=None):
    vmem = pl.BlockSpec(memory_space=pltpu.VMEM)
    smem = pl.BlockSpec(memory_space=pltpu.SMEM)
    specs = [smem] * scalars + [vmem] * (len(args) - scalars) if in_specs is None else in_specs
    return pl.pallas_call(
        body,
        out_shape=out_shape,
        in_specs=specs,
        out_specs=jax.tree.map(lambda _: vmem, out_shape),
        scratch_shapes=list(scratch),
        input_output_aliases=aliases or {},
        compiler_params=pltpu.CompilerParams(vmem_limit_bytes=VMEM_LIMIT),
        cost_estimate=cost,
        name=name,
    )(*args)


def estimate(flops, nbytes):
    return pl.CostEstimate(flops=int(flops), transcendentals=0, bytes_accessed=int(nbytes))


def dot(a, b):
    return jnp.dot(a, b, preferred_element_type=f32)


def dot_last(a, b):
    return lax.dot_general(a, b, (((1,), (1,)), ((), ())), preferred_element_type=f32)


def expand_taps(w_ref, wexp, blocks):
    for c in range(blocks):
        for k in range(w_ref.shape[0]):
            row = w_ref[k : k + 1, c * LANES : (c + 1) * LANES].astype(f32)
            wexp[c, k] = jnp.broadcast_to(row, (8, LANES))


def zero_edges(buf, blocks, rows, cols):
    zero = jnp.zeros((rows, EDGE, LANES), f32)
    for c in range(blocks):
        buf[c, :, 0:EDGE, :] = zero
        buf[c, :, EDGE + cols : EDGE + cols + EDGE, :] = zero


def conv_block(src, c, wexp, rows, start, width, flip):
    groups = width // 8
    acc = [None] * rows
    for j in range(7):
        at = start + EDGE + (3 - j if flip else j - 3)
        for hp in range(rows):
            piece = src[c, hp, at : at + width, :].reshape(groups, 8, LANES)
            for h in range(max(0, hp - 3), min(rows, hp + 4)):
                i = h - hp + 3 if flip else hp - h + 3
                term = piece * wexp[c, 7 * i + j]
                acc[h] = term if acc[h] is None else acc[h] + term
    return acc


def front_kernel(x_ref, g_ref, w_ref, db_ref, gain_ref, shift_ref, scale_ref,
                 yn_ref, gp_ref, gpt_ref, normed_ref, rstd_ref, xp_ref, sums_ref, wexp):
    rows, cols, chans = x_ref.shape
    blocks = chans // LANES
    half = cols // 2
    zero_edges(xp_ref, blocks, rows, cols)
    for c in range(blocks):
        xp_ref[c, :, EDGE : EDGE + cols, :] = x_ref[:, :, c * LANES : (c + 1) * LANES].astype(f32)
    expand_taps(w_ref, wexp, blocks)

    def conv_step(c, carry):
        lanes = pl.ds(pl.multiple_of(c * LANES, LANES), LANES)
        for part in range(2):
            acc = conv_block(xp_ref, c, wexp, rows, part * half, half, False)
            for h in range(rows):
                normed_ref[h * cols + part * half : h * cols + part * half + half, lanes] = acc[h].reshape(half, LANES)
        return carry

    lax.fori_loop(0, blocks, conv_step, 0)
    bias, gain, shift, scale = db_ref[...], gain_ref[...], shift_ref[...], scale_ref[...]

    def norm_step(r, carry):
        at = pl.ds(pl.multiple_of(r * cols, cols), cols)
        d = normed_ref[at, :] + bias
        d = d - jnp.mean(d, axis=-1, keepdims=True)
        rs = lax.rsqrt(jnp.mean(d * d, axis=-1, keepdims=True) + 1e-06)
        normed = d * rs
        normed_ref[at, :] = normed
        rstd_ref[at, :] = jnp.broadcast_to(rs, (cols, LANES))
        yn_ref[at, :] = (normed * gain + shift).astype(bf16)
        g = g_ref[r].astype(f32)
        gp = (g * scale).astype(bf16)
        gp_ref[at, :] = gp
        b2 = jnp.sum(gp.astype(f32).reshape(cols // 8, 8, chans), axis=0)
        gs = jnp.sum(g.reshape(cols // 8, 8, chans), axis=0)
        return carry[0] + b2, carry[1] + gs

    zero = jnp.zeros((8, chans), f32)
    b2, gs = lax.fori_loop(0, rows, norm_step, (zero, zero))
    sums_ref[0:1, :] = jnp.sum(b2, axis=0, keepdims=True)
    sums_ref[1:2, :] = jnp.sum(gs, axis=0, keepdims=True)
    sums_ref[2:8, :] = jnp.zeros((6, chans), f32)
    gpt_ref[...] = gp_ref[...].T


def wide_kernel(pos_ref, yn_ref, gp_ref, w1_ref, b1_ref, w2_ref, *rest, first):
    if first:
        gn_ref, bsum_ref, kh_ref, kg_ref, sh_ref, sg_ref = rest
        gin_ref = None
    else:
        gin_ref, gn_ref, bsum_ref, kh_ref, kg_ref, sh_ref, sg_ref = rest
    cells = yn_ref.shape[0]
    wide = bsum_ref.shape[1]
    part = wide // 2
    at = pl.multiple_of(pos_ref[0] * wide, wide)
    core = pos_ref[1]
    w1 = w1_ref[pl.ds(at, wide), :]
    w2 = w2_ref[:, pl.ds(at, wide)]
    b1 = b1_ref[:, pl.ds(at, wide)]
    step = 128
    total = jnp.zeros((8, wide), f32)
    for r in range(0, cells, step):
        pre = dot_last(yn_ref[r : r + step, :], w1) + b1
        cdf = 0.5 * (1.0 + lax.erf(pre * root_half))
        hidden = (pre * cdf).astype(bf16)
        ghid = dot(gp_ref[r : r + step, :], w2)
        density = jnp.exp(-0.5 * pre * pre) * inv_root_two_pi
        gpre = (ghid * (cdf + pre * density)).astype(bf16)
        total = total + jnp.sum(gpre.astype(f32).reshape(step // 8, 8, wide), axis=0)
        gn = dot(gpre, w1)
        gn_ref[r : r + step, :] = gn if first else gin_ref[r : r + step, :] + gn
        gt = gpre.T
        for side in range(2):
            @pl.when(core == side)
            def _(side=side):
                k, s = side * part, (1 - side) * part
                kh_ref[r : r + step, :] = hidden[:, k : k + part]
                sh_ref[r : r + step, :] = hidden[:, s : s + part]
                kg_ref[:, r : r + step] = gt[k : k + part, :]
                sg_ref[:, r : r + step] = gt[s : s + part, :]
    bsum_ref[...] = jnp.broadcast_to(jnp.sum(total, axis=0, keepdims=True), (8, wide))


def share_kernel(pos_ref, w2_ref, yo_ref, ys_ref, go_ref, gs_ref, kh_ref, rh_ref, kg_ref, rg_ref,
                 d1_ref, d2_ref, scale_ref):
    part = kh_ref.shape[1]
    at = pl.multiple_of((2 * pos_ref[0] + pos_ref[1]) * part, part)
    d1 = dot(kg_ref[...], yo_ref[...]) + dot(rg_ref[...], ys_ref[...])
    d1_ref[...] = d1.astype(d1_ref.dtype)
    d2 = dot(go_ref[...], kh_ref[...]) + dot(gs_ref[...], rh_ref[...])
    d2_ref[...] = d2.astype(d2_ref.dtype)
    prod = d2 * w2_ref[:, pl.ds(at, part)].astype(f32)
    lanes = prod[:, 0:LANES]
    for k in range(LANES, part, LANES):
        lanes = lanes + prod[:, k : k + LANES]
    scale_ref[...] = lanes


def back_kernel(gn_ref, normed_ref, rstd_ref, gain_ref, g_ref, w_ref, gi_ref, gd_ref, sums_ref, wexp):
    rows, cols, chans = g_ref.shape
    blocks = chans // LANES
    half = cols // 2
    zero_edges(gd_ref, blocks, rows, cols)
    expand_taps(w_ref, wexp, blocks)
    gain = gain_ref[...]

    def norm_step(r, carry):
        at = pl.ds(pl.multiple_of(r * cols, cols), cols)
        gn = gn_ref[at, :]
        normed = normed_ref[at, :]
        prod = gn * normed
        scaled = gn * gain
        mean_a = jnp.mean(scaled, axis=-1, keepdims=True)
        mean_b = jnp.mean(prod * gain, axis=-1, keepdims=True)
        rs = rstd_ref[at, 0:1]
        gd = rs * (scaled - mean_a - normed * mean_b)
        for c in range(blocks):
            gd_ref[c, r, EDGE : EDGE + cols, :] = gd[:, c * LANES : (c + 1) * LANES]
        fold = lambda v: jnp.sum(v.reshape(cols // 8, 8, chans), axis=0)
        return carry[0] + fold(gd), carry[1] + fold(prod), carry[2] + fold(gn)

    zero = jnp.zeros((8, chans), f32)
    sums = lax.fori_loop(0, rows, norm_step, (zero, zero, zero))
    for k in range(3):
        sums_ref[k : k + 1, :] = jnp.sum(sums[k], axis=0, keepdims=True)
    sums_ref[3:8, :] = jnp.zeros((5, chans), f32)

    def conv_step(c, carry):
        lanes = pl.ds(pl.multiple_of(c * LANES, LANES), LANES)
        for part in range(2):
            acc = conv_block(gd_ref, c, wexp, rows, part * half, half, True)
            for h in range(rows):
                span = slice(part * half, part * half + half)
                gi_ref[h, span, lanes] = (g_ref[h, span, lanes].astype(f32) + acc[h].reshape(half, LANES)).astype(bf16)
        return carry

    lax.fori_loop(0, blocks, conv_step, 0)


def tap_kernel(xp_ref, gd_ref, taps_ref):
    blocks, rows, padded, _ = xp_ref.shape
    cols = padded - 2 * EDGE

    def step(c, carry):
        lanes = pl.ds(pl.multiple_of(c * LANES, LANES), LANES)
        for j in range(7):
            acc = [None] * 7
            for b in range(0, cols, 16):
                grads = [gd_ref[c, h, EDGE + b : EDGE + b + 16, :].reshape(2, 8, LANES) for h in range(rows)]
                for hp in range(rows):
                    at = EDGE + b + j - 3
                    piece = xp_ref[c, hp, at : at + 16, :].reshape(2, 8, LANES)
                    for h in range(max(0, hp - 3), min(rows, hp + 4)):
                        i = hp - h + 3
                        term = grads[h] * piece
                        term = term[0] + term[1]
                        acc[i] = term if acc[i] is None else acc[i] + term
            for i in range(7):
                taps_ref[7 * i + j : 7 * i + j + 1, lanes] = jnp.sum(acc[i], axis=0, keepdims=True)
        return carry

    lax.fori_loop(0, blocks, step, 0)


def shifted(block, axis, distance):
    devices = range(lax.axis_size(axis))
    route = [(i - distance, i) for i in devices if i - distance in devices]
    return lax.ppermute(block, axis, route)


def swap(value, bit, count):
    return lax.ppermute(value, "dp", [(i, i ^ bit) for i in range(count)])


def shards(
    block_input,
    grad_output,
    depth_weight,
    depth_bias,
    norm_gain,
    norm_shift,
    pw1_weight,
    pw1_bias,
    pw2_weight,
    pw2_bias,
    layer_scale,
):
    x, g = block_input[0, 0], grad_output[0, 0]
    rows, cols, chans = x.shape
    cells = rows * cols
    blocks = chans // LANES
    taps = depth_weight.shape[1]
    w1, w2 = pw1_weight[0], pw2_weight[0]
    units = w1.shape[0]
    replicas = lax.axis_size("dp")
    factor = 1.0 / replicas
    wide = 768
    part = wide // 2
    me = lax.axis_index("dp")
    chip, core = me // 2, me % 2

    wexp = pltpu.VMEM((blocks, taps, 8, LANES), f32)
    padded = struct((blocks, rows, cols + 2 * EDGE, LANES), f32)
    yn, gp, gpt, normed, rstd, xp, sums_a = call(
        front_kernel,
        (struct((cells, chans), bf16), struct((cells, chans), bf16), struct((chans, cells), bf16),
         struct((cells, chans), f32), struct((cells, LANES), f32), padded, struct((8, chans), f32)),
        x, g, depth_weight[0], depth_bias, norm_gain, norm_shift, layer_scale,
        name="front", scratch=[wexp], cost=estimate(1e10, 5e6),
    )

    def wide_step(p, gn):
        pos = jnp.stack([p, core]).astype(jnp.int32)
        outs = (struct((cells, chans), f32), struct((8, wide), f32), struct((cells, part), bf16),
                struct((part, cells), bf16), struct((cells, part), bf16), struct((part, cells), bf16))
        first = gn is None
        args = (pos, yn, gp, w1, pw1_bias, w2) + (() if first else (gn,))
        return call(
            lambda *refs: wide_kernel(*refs, first=first), outs, *args,
            name="wide", aliases={} if first else {6: 0}, scalars=1, cost=estimate(4e9, 8e6),
        )

    if replicas == 8 and units == 4 * wide:
        yn_s, gpt_s = swap(yn, 1, replicas), swap(gpt, 1, replicas)

        def share(p, kh, kg, rh, rg, types):
            pos = jnp.stack([p, core]).astype(jnp.int32)
            outs = (struct((part, chans), types[0]), struct((chans, part), types[1]), struct((chans, LANES), f32))
            return call(share_kernel, outs, pos, w2, yn, yn_s, gpt, gpt_s, kh, rh, kg, rg,
                        name="share", scalars=1, cost=estimate(2e9, 5e6))

        pd, px, py = chip ^ 3, chip ^ 1, chip ^ 2
        gn, bd, khd, kgd, shd, sgd = wide_step(pd, None)
        rhd, rgd = swap(shd, 1, replicas), swap(sgd, 1, replicas)
        gn, bx, khx, kgx, shx, sgx = wide_step(px, gn)
        rhx, rgx = swap(shx, 1, replicas), swap(sgx, 1, replicas)
        d1, d2, sc_d = share(pd, khd, kgd, rhd, rgd, (bf16, bf16))
        gn, d1, d2 = lax.optimization_barrier((gn, d1, d2))
        d1_in, d2_in = swap(d1, 2, replicas), swap(d2, 4, replicas)
        gn, by, khy, kgy, shy, sgy = wide_step(py, gn)
        rhy, rgy = swap(shy, 1, replicas), swap(sgy, 1, replicas)
        x1, x2, sc_x = share(px, khx, kgx, rhx, rgx, (bf16, f32))
        gn, x1, x2 = lax.optimization_barrier((gn, x1, x2))
        x1_in = swap(x1, 2, replicas)
        gn, bo, kho, kgo, sho, sgo = wide_step(chip, gn)
        rho, rgo = swap(sho, 1, replicas), swap(sgo, 1, replicas)
        y1, y2, sc_y = share(py, khy, kgy, rhy, rgy, (f32, bf16))
        gn, y1, y2 = lax.optimization_barrier((gn, y1, y2))
        y2_in = swap(y2, 4, replicas)
    else:
        gn, bsums, scales, g1, g2 = None, [], [], [], []
        for p in range(units // wide):
            gn, bsum, kh, kg, sh, sg = wide_step(jnp.int32(p), gn)
            lo = lambda k, s: jnp.where(core == 0, k, s)
            hidden = jnp.concatenate([lo(kh, sh), lo(sh, kh)], axis=1)
            gpre_t = jnp.concatenate([lo(kg, sg), lo(sg, kg)], axis=0)
            bsums.append(bsum[0])
            g1.append(dot(gpre_t, yn))
            g2.append(dot(gpt, hidden))
        g1, g2 = jnp.concatenate(g1, axis=0), jnp.concatenate(g2, axis=1)
        scale_sum = jnp.sum(g2 * w2.astype(f32), axis=1)
        b1_sum = jnp.concatenate(bsums)

    gi, gd, sums_b = call(
        back_kernel,
        (struct((rows, cols, chans), bf16), padded, struct((8, chans), f32)),
        gn, normed, rstd, norm_gain, g, depth_weight[0],
        name="back", scratch=[wexp], cost=estimate(1e10, 6e6),
    )
    received = shifted(gi, "section", -1)

    if replicas == 8 and units == 4 * wide:
        o1, o2, sc_o = share(chip, kho, kgo, rho, rgo, (f32, f32))
        scale_sum = jnp.sum(sc_d + sc_x + sc_y + sc_o, axis=1)
        pieces = jnp.stack([bo[0], bx[0], by[0], bd[0]])
        b1_sum = jnp.concatenate([lax.dynamic_slice(pieces, (chip ^ k, 0), (1, wide))[0] for k in range(4)])

    tap_term = call(tap_kernel, struct((taps, chans), f32), xp, gd, name="taps", cost=estimate(1e10, 4e6))
    gscale = scale_sum / layer_scale[0] + pw2_bias[0] * sums_a[1]
    small = jnp.concatenate([tap_term, sums_b[0:3], sums_a[0:1], gscale[None], b1_sum.reshape(-1, chans)], axis=0)

    if replicas == 8 and units == 4 * wide:
        m2 = (x2 + d2_in.astype(f32)).astype(bf16)
        m1 = (y1 + d1_in.astype(f32)).astype(bf16)
        m2_in, m1_in = swap(m2, 2, replicas), swap(m1, 4, replicas)
        for bit in (1, 2, 4):
            small = small + swap(small, bit, replicas)
        out1 = o1 + x1_in.astype(f32) + m1_in.astype(f32)
        out2 = o2 + y2_in.astype(f32) + m2_in.astype(f32)
    else:
        small = lax.psum(small, "dp")
        out1 = lax.psum_scatter(g1, "dp", scatter_dimension=0, tiled=True)
        out2 = lax.psum_scatter(g2, "dp", scatter_dimension=1, tiled=True)
    small = small * factor
    return (
        (out1 * factor)[None],
        (out2 * factor)[None],
        small[taps + 5 :].reshape(1, -1),
        small[None, : taps + 5],
        received[None, None],
    )


def solution(mesh):
    in_specs = (
        P("section", "dp", None, None, None),
        P("section", "dp", None, None, None),
        P("section", None, None),
        P("section", None),
        P("section", None),
        P("section", None),
        P("section", None, None),
        P("section", None),
        P("section", None, None),
        P("section", None),
        P("section", None),
    )
    out_specs = (
        P("section", "dp", None),
        P("section", None, "dp"),
        P("section", None),
        P("section", None, None),
        P("section", "dp", None, None, None),
    )
    return jax.shard_map(shards, mesh=mesh, in_specs=in_specs, out_specs=out_specs, check_vma=False)
```

```python
import jax
import jax.numpy as jnp
from jax import lax
from jax.experimental import pallas as pl
from jax.experimental.pallas import tpu as pltpu
from jax.sharding import PartitionSpec as P

root_half = 0.7071067811865476
inv_root_two_pi = 0.3989422804014327
f32 = jnp.float32
bf16 = jnp.bfloat16
LANES = 128
EDGE = 8
VMEM_LIMIT = 12 * 1024 * 1024


def struct(shape, dtype):
    return jax.ShapeDtypeStruct(shape, dtype)


def call(body, out_shape, *args, name, aliases=None, scratch=(), scalars=0, in_specs=None, cost=None):
    vmem = pl.BlockSpec(memory_space=pltpu.VMEM)
    smem = pl.BlockSpec(memory_space=pltpu.SMEM)
    specs = [smem] * scalars + [vmem] * (len(args) - scalars) if in_specs is None else in_specs
    return pl.pallas_call(
        body,
        out_shape=out_shape,
        in_specs=specs,
        out_specs=jax.tree.map(lambda _: vmem, out_shape),
        scratch_shapes=list(scratch),
        input_output_aliases=aliases or {},
        compiler_params=pltpu.CompilerParams(vmem_limit_bytes=VMEM_LIMIT),
        cost_estimate=cost,
        name=name,
    )(*args)


def estimate(flops, nbytes):
    return pl.CostEstimate(flops=int(flops), transcendentals=0, bytes_accessed=int(nbytes))


def dot(a, b):
    return jnp.dot(a, b, preferred_element_type=f32)


def dot_last(a, b):
    return lax.dot_general(a, b, (((1,), (1,)), ((), ())), preferred_element_type=f32)


def place():
    me = lax.axis_index("dp")
    return lax.shift_right_logical(me, 1), lax.bitwise_and(me, 1)


def expand_taps(w_ref, wexp, blocks):
    for c in range(blocks):
        for k in range(w_ref.shape[0]):
            row = w_ref[k : k + 1, c * LANES : (c + 1) * LANES].astype(f32)
            wexp[c, k] = jnp.broadcast_to(row, (8, LANES))


def zero_edges(buf, blocks, rows, cols):
    zero = jnp.zeros((rows, EDGE, LANES), f32)
    for c in range(blocks):
        buf[c, :, 0:EDGE, :] = zero
        buf[c, :, EDGE + cols : EDGE + cols + EDGE, :] = zero


def conv_block(src, c, wexp, rows, start, width, flip):
    groups = width // 8
    acc = [None] * rows
    for j in range(7):
        at = start + EDGE + (3 - j if flip else j - 3)
        for hp in range(rows):
            piece = src[c, hp, at : at + width, :].reshape(groups, 8, LANES)
            for h in range(max(0, hp - 3), min(rows, hp + 4)):
                i = h - hp + 3 if flip else hp - h + 3
                term = piece * wexp[c, 7 * i + j]
                acc[h] = term if acc[h] is None else acc[h] + term
    return acc


def front_kernel(x_hbm, g_hbm, w_hbm, db_hbm, gain_hbm, shift_hbm, scale_hbm, bb_hbm, w1_hbm, b1_hbm, w2_hbm,
                 acts_ref, normed_ref, rstd_ref, xp_ref, vecs_ref, wexp, g_ref, w1_ref, b1_ref, w2_ref,
                 x_ref, w_ref, tmp_ref, sems):
    rows, cols, chans = x_ref.shape
    blocks = chans // LANES
    half = cols // 2
    moves = [(x_hbm, x_ref), (w_hbm, w_ref), (g_hbm, g_ref), (db_hbm, tmp_ref.at[0:1]), (gain_hbm, tmp_ref.at[1:2]),
             (shift_hbm, tmp_ref.at[2:3]), (scale_hbm, tmp_ref.at[3:4]), (bb_hbm, tmp_ref.at[4:5]),
             (w1_hbm, w1_ref), (b1_hbm, b1_ref), (w2_hbm, w2_ref)]
    copies = [pltpu.make_async_copy(src, dst, sems.at[k]) for k, (src, dst) in enumerate(moves)]
    for copy in copies:
        copy.start()
    zero_edges(xp_ref, blocks, rows, cols)
    copies[0].wait()
    for c in range(blocks):
        xp_ref[c, :, EDGE : EDGE + cols, :] = x_ref[:, :, c * LANES : (c + 1) * LANES].astype(f32)
    copies[1].wait()
    expand_taps(w_ref, wexp, blocks)

    def conv_step(c, carry):
        lanes = pl.ds(pl.multiple_of(c * LANES, LANES), LANES)
        for part in range(2):
            acc = conv_block(xp_ref, c, wexp, rows, part * half, half, False)
            for h in range(rows):
                normed_ref[h * cols + part * half : h * cols + part * half + half, lanes] = acc[h].reshape(half, LANES)
        return carry

    lax.fori_loop(0, blocks, conv_step, 0)
    for copy in copies[2:8]:
        copy.wait()
    bias, gain, shift, scale = (tmp_ref[k : k + 1, :] for k in range(4))

    def norm_step(r, carry):
        at = pl.ds(pl.multiple_of(r * cols, cols), cols)
        d = normed_ref[at, :] + bias
        d = d - jnp.mean(d, axis=-1, keepdims=True)
        rs = lax.rsqrt(jnp.mean(d * d, axis=-1, keepdims=True) + 1e-06)
        normed = d * rs
        normed_ref[at, :] = normed
        rstd_ref[at, :] = jnp.broadcast_to(rs, (cols, LANES))
        acts_ref[at, :] = (normed * gain + shift).astype(bf16)
        g = g_ref[r].astype(f32)
        gp = (g * scale).astype(bf16)
        acts_ref[pl.ds(pl.multiple_of((rows + r) * cols, cols), cols), :] = gp
        b2 = jnp.sum(gp.astype(f32).reshape(cols // 8, 8, chans), axis=0)
        gs = jnp.sum(g.reshape(cols // 8, 8, chans), axis=0)
        return carry[0] + b2, carry[1] + gs

    zero = jnp.zeros((8, chans), f32)
    b2, gs = lax.fori_loop(0, rows, norm_step, (zero, zero))
    vecs_ref[0:1, :] = gain
    vecs_ref[1:2, :] = scale
    vecs_ref[2:3, :] = tmp_ref[4:5, :]
    vecs_ref[3:4, :] = jnp.sum(b2, axis=0, keepdims=True)
    vecs_ref[4:5, :] = jnp.sum(gs, axis=0, keepdims=True)
    vecs_ref[5:8, :] = jnp.zeros((3, chans), f32)
    for copy in copies[8:]:
        copy.wait()


def wide_kernel(acts_ref, w1_ref, b1_ref, w2_ref, *rest, first, slot):
    *gin, gn_ref, bsum_ref, keep_ref, send_ref = rest
    cells = acts_ref.shape[0] // 2
    wide = bsum_ref.shape[1]
    part = wide // 2
    chip, core = place()
    at = pl.multiple_of(slot(chip) * wide, wide)
    w1 = w1_ref[pl.ds(at, wide), :]
    w2 = w2_ref[:, pl.ds(at, wide)]
    b1 = b1_ref[:, pl.ds(at, wide)]
    step = 128
    total = jnp.zeros((8, wide), f32)
    for r in range(0, cells, step):
        pre = dot_last(acts_ref[r : r + step, :], w1) + b1
        cdf = 0.5 * (1.0 + lax.erf(pre * root_half))
        hidden = (pre * cdf).astype(bf16)
        ghid = dot(acts_ref[cells + r : cells + r + step, :], w2)
        density = jnp.exp(-0.5 * pre * pre) * inv_root_two_pi
        gpre = (ghid * (cdf + pre * density)).astype(bf16)
        total = total + jnp.sum(gpre.astype(f32).reshape(step // 8, 8, wide), axis=0)
        gn = dot(gpre, w1)
        gn_ref[r : r + step, :] = gn if first else gin[0][r : r + step, :] + gn
        gt, ht = gpre.T, hidden.T
        for side in range(2):
            @pl.when(core == side)
            def _(side=side):
                k, s = side * part, (1 - side) * part
                keep_ref[0:part, r : r + step] = gt[k : k + part, :]
                send_ref[0:part, r : r + step] = gt[s : s + part, :]
                keep_ref[part:, r : r + step] = ht[k : k + part, :]
                send_ref[part:, r : r + step] = ht[s : s + part, :]
    bsum_ref[...] = jnp.broadcast_to(jnp.sum(total, axis=0, keepdims=True), (8, wide))


def share_kernel(w2_ref, own_ref, sib_ref, keep_ref, got_ref, *rest, slot, mode):
    part = keep_ref.shape[0] // 2
    cells = own_ref.shape[0] // 2
    chip, core = place()
    at = pl.multiple_of((2 * slot(chip) + core) * part, part)
    d1 = dot(keep_ref[0:part, :], own_ref[0:cells, :]) + dot(got_ref[0:part, :], sib_ref[0:cells, :])
    d2 = dot(keep_ref[part:, :], own_ref[cells:, :]) + dot(got_ref[part:, :], sib_ref[cells:, :])
    prod = d2 * w2_ref[:, pl.ds(at, part)].T.astype(f32)
    if mode == "split":
        d1_ref, d2_ref, scale_ref = rest
        d1_ref[...] = d1.astype(d1_ref.dtype)
        d2_ref[...] = d2.astype(d2_ref.dtype)
    else:
        in_ref, pack_ref, scale_ref = rest
        more = in_ref[...].astype(f32)
        if mode == "first":
            d1 = d1 + more
        else:
            d2 = d2 + more
        pack_ref[0:part, :] = d1.astype(bf16)
        pack_ref[part:, :] = d2.astype(bf16)
    scale_ref[...] = jnp.sum(prod.reshape(part // 8, 8, prod.shape[1]), axis=0)


def back_kernel(gn_ref, normed_ref, rstd_ref, vecs_ref, g_ref, wexp, gi_ref, gd_ref, sums_ref):
    rows, cols, chans = g_ref.shape
    blocks = chans // LANES
    half = cols // 2
    zero_edges(gd_ref, blocks, rows, cols)
    gain = vecs_ref[0:1, :]

    def norm_step(r, carry):
        at = pl.ds(pl.multiple_of(r * cols, cols), cols)
        gn = gn_ref[at, :]
        normed = normed_ref[at, :]
        prod = gn * normed
        scaled = gn * gain
        mean_a = jnp.mean(scaled, axis=-1, keepdims=True)
        mean_b = jnp.mean(prod * gain, axis=-1, keepdims=True)
        rs = rstd_ref[at, 0:1]
        gd = rs * (scaled - mean_a - normed * mean_b)
        for c in range(blocks):
            gd_ref[c, r, EDGE : EDGE + cols, :] = gd[:, c * LANES : (c + 1) * LANES]
        fold = lambda v: jnp.sum(v.reshape(cols // 8, 8, chans), axis=0)
        return carry[0] + fold(gd), carry[1] + fold(prod), carry[2] + fold(gn)

    zero = jnp.zeros((8, chans), f32)
    sums = lax.fori_loop(0, rows, norm_step, (zero, zero, zero))
    for k in range(3):
        sums_ref[k : k + 1, :] = jnp.sum(sums[k], axis=0, keepdims=True)
    sums_ref[3:8, :] = jnp.zeros((5, chans), f32)

    def conv_step(c, carry):
        lanes = pl.ds(pl.multiple_of(c * LANES, LANES), LANES)
        for part in range(2):
            acc = conv_block(gd_ref, c, wexp, rows, part * half, half, True)
            for h in range(rows):
                span = slice(part * half, part * half + half)
                gi_ref[h, span, lanes] = (g_ref[h, span, lanes].astype(f32) + acc[h].reshape(half, LANES)).astype(bf16)
        return carry

    lax.fori_loop(0, blocks, conv_step, 0)


def tap_kernel(xp_ref, gd_ref, vecs_ref, sums_ref, *rest, taps, fast):
    *more, small_ref = rest
    blocks, rows, padded, _ = xp_ref.shape
    cols = padded - 2 * EDGE
    chans = blocks * LANES

    def step(c, carry):
        lanes = pl.ds(pl.multiple_of(c * LANES, LANES), LANES)
        for j in range(7):
            acc = [None] * 7
            for b in range(0, cols, 16):
                grads = [gd_ref[c, h, EDGE + b : EDGE + b + 16, :].reshape(2, 8, LANES) for h in range(rows)]
                for hp in range(rows):
                    at = EDGE + b + j - 3
                    piece = xp_ref[c, hp, at : at + 16, :].reshape(2, 8, LANES)
                    for h in range(max(0, hp - 3), min(rows, hp + 4)):
                        i = hp - h + 3
                        term = grads[h] * piece
                        term = term[0] + term[1]
                        acc[i] = term if acc[i] is None else acc[i] + term
            for i in range(7):
                small_ref[7 * i + j : 7 * i + j + 1, lanes] = jnp.sum(acc[i], axis=0, keepdims=True)
        return carry

    small_ref[taps:, :] = jnp.zeros((small_ref.shape[0] - taps, chans), f32)
    lax.fori_loop(0, blocks, step, 0)
    small_ref[taps : taps + 3, :] = sums_ref[0:3, :]
    small_ref[taps + 3 : taps + 4, :] = vecs_ref[3:4, :]
    if fast:
        scales, bsums = more[:4], more[4:]
        total = scales[0][...] + scales[1][...] + scales[2][...] + scales[3][...]
        row = jnp.sum(total, axis=0, keepdims=True) / vecs_ref[1:2, :] + vecs_ref[2:3, :] * vecs_ref[4:5, :]
        small_ref[taps + 4 : taps + 5, :] = row
        chip, _ = place()
        for k in range(4):
            small_ref[pl.ds(taps + 5 + lax.bitwise_xor(chip, k), 1), :] = bsums[k][0:1, :]


def merge_kernel(o1_ref, o2_ref, x_ref, y_ref, out1_ref, out2_ref, *, factor):
    part = o1_ref.shape[0]
    out1_ref[...] = (o1_ref[...] + x_ref[0:part, :].astype(f32) + y_ref[0:part, :].astype(f32)) * factor
    out2_ref[...] = ((o2_ref[...] + x_ref[part:, :].astype(f32) + y_ref[part:, :].astype(f32)) * factor).T


def shifted(block, axis, distance):
    devices = range(lax.axis_size(axis))
    route = [(i - distance, i) for i in devices if i - distance in devices]
    return lax.ppermute(block, axis, route)


def swap(value, bit, count):
    return lax.ppermute(value, "dp", [(i, i ^ bit) for i in range(count)])


def shards(
    block_input,
    grad_output,
    depth_weight,
    depth_bias,
    norm_gain,
    norm_shift,
    pw1_weight,
    pw1_bias,
    pw2_weight,
    pw2_bias,
    layer_scale,
):
    x, g = block_input[0, 0], grad_output[0, 0]
    rows, cols, chans = x.shape
    cells = rows * cols
    blocks = chans // LANES
    taps = depth_weight.shape[1]
    w1, w2 = pw1_weight[0], pw2_weight[0]
    units = w1.shape[0]
    replicas = lax.axis_size("dp")
    factor = 1.0 / replicas
    wide = 768
    part = wide // 2
    fast = replicas == 8 and units == 4 * wide

    wexp = struct((blocks, taps, 8, LANES), f32)
    padded = struct((blocks, rows, cols + 2 * EDGE, LANES), f32)
    like = lambda v: struct(v.shape, v.dtype)
    hbm = pl.BlockSpec(memory_space=pltpu.HBM)
    front_args = (x, g, depth_weight[0], depth_bias, norm_gain, norm_shift, layer_scale, pw2_bias, w1, pw1_bias, w2)
    acts, normed, rstd, xp, vecs, wexp, gv, w1, b1, w2 = call(
        front_kernel,
        (struct((2 * cells, chans), bf16), struct((cells, chans), f32), struct((cells, LANES), f32), padded, struct((8, chans), f32), wexp,
         like(g), like(w1), like(pw1_bias), like(w2)),
        *(pltpu.with_memory_space_constraint(v, pltpu.HBM) for v in front_args),
        name="front", in_specs=[hbm] * 11, cost=estimate(1e10, 1e6),
        scratch=[pltpu.VMEM(x.shape, bf16), pltpu.VMEM((taps, chans), bf16), pltpu.VMEM((8, chans), f32),
                 pltpu.SemaphoreType.DMA((11,))],
    )

    def wide_step(slot, gn):
        outs = (struct((cells, chans), f32), struct((8, wide), f32), struct((wide, cells), bf16),
                struct((wide, cells), bf16))
        first = gn is None
        args = (acts, w1, b1, w2) + (() if first else (gn,))
        return call(
            lambda *refs: wide_kernel(*refs, first=first, slot=slot), outs, *args,
            name="wide", aliases={} if first else {4: 0}, cost=estimate(1e10, 1e6),
        )

    def flip(k):
        return lambda chip: lax.bitwise_xor(chip, k)

    if fast:
        acts_s = swap(acts, 1, replicas)

        def share(k, keep, got, types):
            outs = (struct((part, chans), types), struct((part, chans), types), struct((8, chans), f32))
            return call(lambda *refs: share_kernel(*refs, slot=flip(k), mode="split"), outs,
                        w2, acts, acts_s, keep, got, name="share", cost=estimate(1e6, 1e3))

        def share_pack(k, keep, got, more, mode):
            outs = (struct((wide, chans), bf16), struct((8, chans), f32))
            return call(lambda *refs: share_kernel(*refs, slot=flip(k), mode=mode), outs,
                        w2, acts, acts_s, keep, got, more, name="pack", cost=estimate(1e10, 1e6))

        gn, bd, keep_d, send_d = wide_step(flip(3), None)
        got_d = swap(send_d, 1, replicas)
        gn, bx, keep_x, send_x = wide_step(flip(1), gn)
        got_x = swap(send_x, 1, replicas)
        d1, d2, sc_d = share(3, keep_d, got_d, bf16)
        gn, d1, d2 = lax.optimization_barrier((gn, d1, d2))
        d1_in, d2_in = swap(d1, 2, replicas), swap(d2, 4, replicas)
        gn, by, keep_y, send_y = wide_step(flip(2), gn)
        got_y = swap(send_y, 1, replicas)
        gn, bo, keep_o, send_o = wide_step(flip(0), gn)
        got_o = swap(send_o, 1, replicas)
        pack_x, sc_x = share_pack(1, keep_x, got_x, d2_in, "second")
        gn, pack_x, d1_in = lax.optimization_barrier((gn, pack_x, d1_in))
        pack_y, sc_y = share_pack(2, keep_y, got_y, d1_in, "first")
        gn, pack_y = lax.optimization_barrier((gn, pack_y))
        x_in, y_in = swap(pack_x, 2, replicas), swap(pack_y, 4, replicas)
    else:
        core = lax.axis_index("dp") % 2
        gn, bsums, g1, g2 = None, [], [], []
        for p in range(units // wide):
            gn, bsum, keep, send = wide_step(lambda chip, p=p: jnp.int32(p), gn)
            lo, hi = jnp.where(core == 0, keep, send), jnp.where(core == 0, send, keep)
            bsums.append(bsum[0:1])
            g1 += [dot(v[:part], acts[:cells]) for v in (lo, hi)]
            g2 += [dot(v[part:], acts[cells:]) for v in (lo, hi)]
        g1, g2 = jnp.concatenate(g1, axis=0), jnp.concatenate(g2, axis=0).T

    gi, gd, sums = call(
        back_kernel,
        (struct((rows, cols, chans), bf16), padded, struct((8, chans), f32)),
        gn, normed, rstd, vecs, gv, wexp,
        name="back", cost=estimate(1e6, 1e3),
    )
    received = shifted(gi, "section", -1)

    if fast:
        o1, o2, sc_o = share(0, keep_o, got_o, f32)
        more = (sc_d, sc_x, sc_y, sc_o, bo, bx, by, bd)
    else:
        more = ()
    total_rows = -(-(taps + 5 + units // chans) // 8) * 8
    small = call(lambda *refs: tap_kernel(*refs, taps=taps, fast=fast), struct((total_rows, chans), f32),
                 xp, gd, vecs, sums, *more, name="taps", cost=estimate(1e6, 1e3))

    if fast:
        for bit in (1, 2, 4):
            small = small + swap(small, bit, replicas)
        out1, out2 = call(
            lambda *refs: merge_kernel(*refs, factor=factor),
            (struct((part, chans), f32), struct((chans, part), f32)),
            o1, o2, x_in, y_in, name="merge", cost=estimate(1e10, 1e6),
        )
    else:
        scale_sum = jnp.sum(g2 * w2.astype(f32), axis=1)
        gscale = scale_sum / layer_scale[0] + pw2_bias[0] * vecs[4]
        small = jnp.concatenate([small[: taps + 4], gscale[None], *bsums], axis=0)
        small = lax.psum(small, "dp")
        out1 = lax.psum_scatter(g1, "dp", scatter_dimension=0, tiled=True) * factor
        out2 = lax.psum_scatter(g2, "dp", scatter_dimension=1, tiled=True) * factor
    small = small * factor
    return (
        out1[None],
        out2[None],
        small[taps + 5 : taps + 5 + units // chans].reshape(1, -1),
        small[None, : taps + 5],
        received[None, None],
    )


def solution(mesh):
    in_specs = (
        P("section", "dp", None, None, None),
        P("section", "dp", None, None, None),
        P("section", None, None),
        P("section", None),
        P("section", None),
        P("section", None),
        P("section", None, None),
        P("section", None),
        P("section", None, None),
        P("section", None),
        P("section", None),
    )
    out_specs = (
        P("section", "dp", None),
        P("section", None, "dp"),
        P("section", None),
        P("section", None, None),
        P("section", "dp", None, None, None),
    )
    return jax.shard_map(shards, mesh=mesh, in_specs=in_specs, out_specs=out_specs, check_vma=False)
```

```python
import jax
import jax.numpy as jnp
from jax import lax
from jax.experimental import pallas as pl
from jax.experimental.pallas import tpu as pltpu
from jax.sharding import PartitionSpec as P

root_half = 0.7071067811865476
inv_root_two_pi = 0.3989422804014327
f32 = jnp.float32
bf16 = jnp.bfloat16
LANES = 128
EDGE = 8
VMEM_LIMIT = 12 * 1024 * 1024


def struct(shape, dtype):
    return jax.ShapeDtypeStruct(shape, dtype)


def call(body, out_shape, *args, name, aliases=None, scratch=(), scalars=0, in_specs=None, cost=None):
    vmem = pl.BlockSpec(memory_space=pltpu.VMEM)
    smem = pl.BlockSpec(memory_space=pltpu.SMEM)
    specs = [smem] * scalars + [vmem] * (len(args) - scalars) if in_specs is None else in_specs
    return pl.pallas_call(
        body,
        out_shape=out_shape,
        in_specs=specs,
        out_specs=jax.tree.map(lambda _: vmem, out_shape),
        scratch_shapes=list(scratch),
        input_output_aliases=aliases or {},
        compiler_params=pltpu.CompilerParams(vmem_limit_bytes=VMEM_LIMIT),
        cost_estimate=cost,
        name=name,
    )(*args)


def estimate(flops, nbytes):
    return pl.CostEstimate(flops=int(flops), transcendentals=0, bytes_accessed=int(nbytes))


def dot(a, b):
    return jnp.dot(a, b, preferred_element_type=f32)


def dot_last(a, b):
    return lax.dot_general(a, b, (((1,), (1,)), ((), ())), preferred_element_type=f32)


def place():
    me = lax.axis_index("dp")
    return lax.shift_right_logical(me, 1), lax.bitwise_and(me, 1)


def expand_taps(w_ref, wexp, blocks):
    for c in range(blocks):
        for k in range(w_ref.shape[0]):
            row = w_ref[k : k + 1, c * LANES : (c + 1) * LANES].astype(f32)
            wexp[c, k] = jnp.broadcast_to(row, (8, LANES))


def zero_edges(buf, blocks, rows, cols):
    zero = jnp.zeros((rows, EDGE, LANES), f32)
    for c in range(blocks):
        buf[c, :, 0:EDGE, :] = zero
        buf[c, :, EDGE + cols : EDGE + cols + EDGE, :] = zero


def conv_block(src, c, wexp, rows, start, width, flip):
    groups = width // 8
    acc = [None] * rows
    for j in range(7):
        at = start + EDGE + (3 - j if flip else j - 3)
        for hp in range(rows):
            piece = src[c, hp, at : at + width, :].reshape(groups, 8, LANES)
            for h in range(max(0, hp - 3), min(rows, hp + 4)):
                i = h - hp + 3 if flip else hp - h + 3
                term = piece * wexp[c, 7 * i + j]
                acc[h] = term if acc[h] is None else acc[h] + term
    return acc


def front_kernel(x_hbm, g_hbm, w_hbm, db_hbm, gain_hbm, shift_hbm, scale_hbm, bb_hbm, w1_hbm, b1_hbm, w2_hbm,
                 acts_ref, normed_ref, rstd_ref, xp_ref, vecs_ref, wexp, g_ref, w1_ref, b1_ref, w2_ref,
                 x_ref, w_ref, tmp_ref, sems):
    rows, cols, chans = x_ref.shape
    blocks = chans // LANES
    half = cols // 2
    moves = [(x_hbm, x_ref), (w_hbm, w_ref), (g_hbm, g_ref), (db_hbm, tmp_ref.at[0:1]), (gain_hbm, tmp_ref.at[1:2]),
             (shift_hbm, tmp_ref.at[2:3]), (scale_hbm, tmp_ref.at[3:4]), (bb_hbm, tmp_ref.at[4:5]),
             (w1_hbm, w1_ref), (b1_hbm, b1_ref), (w2_hbm, w2_ref)]
    copies = [pltpu.make_async_copy(src, dst, sems.at[k]) for k, (src, dst) in enumerate(moves)]
    for copy in copies:
        copy.start()
    zero_edges(xp_ref, blocks, rows, cols)
    copies[0].wait()
    for c in range(blocks):
        xp_ref[c, :, EDGE : EDGE + cols, :] = x_ref[:, :, c * LANES : (c + 1) * LANES].astype(f32)
    copies[1].wait()
    expand_taps(w_ref, wexp, blocks)

    def conv_step(c, carry):
        lanes = pl.ds(pl.multiple_of(c * LANES, LANES), LANES)
        for part in range(2):
            acc = conv_block(xp_ref, c, wexp, rows, part * half, half, False)
            for h in range(rows):
                normed_ref[h * cols + part * half : h * cols + part * half + half, lanes] = acc[h].reshape(half, LANES)
        return carry

    lax.fori_loop(0, blocks, conv_step, 0)
    for copy in copies[2:8]:
        copy.wait()
    bias, gain, shift, scale = (tmp_ref[k : k + 1, :] for k in range(4))

    def norm_step(r, carry):
        at = pl.ds(pl.multiple_of(r * cols, cols), cols)
        d = normed_ref[at, :] + bias
        d = d - jnp.mean(d, axis=-1, keepdims=True)
        rs = lax.rsqrt(jnp.mean(d * d, axis=-1, keepdims=True) + 1e-06)
        normed = d * rs
        normed_ref[at, :] = normed
        rstd_ref[at, :] = jnp.broadcast_to(rs, (cols, LANES))
        acts_ref[at, :] = (normed * gain + shift).astype(bf16)
        g = g_ref[r].astype(f32)
        gp = (g * scale).astype(bf16)
        acts_ref[pl.ds(pl.multiple_of((rows + r) * cols, cols), cols), :] = gp
        b2 = jnp.sum(gp.astype(f32).reshape(cols // 8, 8, chans), axis=0)
        gs = jnp.sum(g.reshape(cols // 8, 8, chans), axis=0)
        return carry[0] + b2, carry[1] + gs

    zero = jnp.zeros((8, chans), f32)
    b2, gs = lax.fori_loop(0, rows, norm_step, (zero, zero))
    vecs_ref[0:1, :] = gain
    vecs_ref[1:2, :] = scale
    vecs_ref[2:3, :] = tmp_ref[4:5, :]
    vecs_ref[3:4, :] = jnp.sum(b2, axis=0, keepdims=True)
    vecs_ref[4:5, :] = jnp.sum(gs, axis=0, keepdims=True)
    vecs_ref[5:8, :] = jnp.zeros((3, chans), f32)
    for copy in copies[8:]:
        copy.wait()


def wide_kernel(acts_ref, w1_ref, b1_ref, w2_ref, *rest, first, slot):
    *gin, gn_ref, bsum_ref, keep_ref, send_ref = rest
    cells = acts_ref.shape[0] // 2
    wide = bsum_ref.shape[1]
    part = wide // 2
    chip, core = place()
    at = pl.multiple_of(slot(chip) * wide, wide)
    w1 = w1_ref[pl.ds(at, wide), :]
    w2 = w2_ref[:, pl.ds(at, wide)]
    b1 = b1_ref[:, pl.ds(at, wide)]
    step = 128
    total = jnp.zeros((8, wide), f32)
    for r in range(0, cells, step):
        pre = dot_last(acts_ref[r : r + step, :], w1) + b1
        cdf = 0.5 * (1.0 + lax.erf(pre * root_half))
        hidden = (pre * cdf).astype(bf16)
        ghid = dot(acts_ref[cells + r : cells + r + step, :], w2)
        density = jnp.exp(-0.5 * pre * pre) * inv_root_two_pi
        gpre = (ghid * (cdf + pre * density)).astype(bf16)
        total = total + jnp.sum(gpre.astype(f32).reshape(step // 8, 8, wide), axis=0)
        gn = dot(gpre, w1)
        gn_ref[r : r + step, :] = gn if first else gin[0][r : r + step, :] + gn
        gt, ht = gpre.T, hidden.T
        for side in range(2):
            @pl.when(core == side)
            def _(side=side):
                k, s = side * part, (1 - side) * part
                keep_ref[0:part, r : r + step] = gt[k : k + part, :]
                send_ref[0:part, r : r + step] = gt[s : s + part, :]
                keep_ref[part:, r : r + step] = ht[k : k + part, :]
                send_ref[part:, r : r + step] = ht[s : s + part, :]
    bsum_ref[...] = jnp.broadcast_to(jnp.sum(total, axis=0, keepdims=True), (8, wide))


def share_kernel(w2_ref, own_ref, sib_ref, keep_ref, got_ref, *rest, slot, mode):
    part = keep_ref.shape[0] // 2
    cells = own_ref.shape[0] // 2
    chip, core = place()
    at = pl.multiple_of((2 * slot(chip) + core) * part, part)
    d1 = dot(keep_ref[0:part, :], own_ref[0:cells, :]) + dot(got_ref[0:part, :], sib_ref[0:cells, :])
    d2 = dot(keep_ref[part:, :], own_ref[cells:, :]) + dot(got_ref[part:, :], sib_ref[cells:, :])
    prod = d2 * w2_ref[:, pl.ds(at, part)].T.astype(f32)
    if mode == "split":
        d1_ref, d2_ref, scale_ref = rest
        d1_ref[...] = d1.astype(d1_ref.dtype)
        d2_ref[...] = d2.astype(d2_ref.dtype)
    else:
        in_ref, pack_ref, scale_ref = rest
        more = in_ref[...].astype(f32)
        if mode == "first":
            d1 = d1 + more
        else:
            d2 = d2 + more
        pack_ref[0:part, :] = d1.astype(bf16)
        pack_ref[part:, :] = d2.astype(bf16)
    scale_ref[...] = jnp.sum(prod.reshape(part // 8, 8, prod.shape[1]), axis=0)


def back_kernel(gn_ref, normed_ref, rstd_ref, vecs_ref, g_ref, wexp, gi_ref, gd_ref, sums_ref):
    rows, cols, chans = g_ref.shape
    blocks = chans // LANES
    half = cols // 2
    zero_edges(gd_ref, blocks, rows, cols)
    gain = vecs_ref[0:1, :]

    def norm_step(r, carry):
        at = pl.ds(pl.multiple_of(r * cols, cols), cols)
        gn = gn_ref[at, :]
        normed = normed_ref[at, :]
        prod = gn * normed
        scaled = gn * gain
        mean_a = jnp.mean(scaled, axis=-1, keepdims=True)
        mean_b = jnp.mean(prod * gain, axis=-1, keepdims=True)
        rs = rstd_ref[at, 0:1]
        gd = rs * (scaled - mean_a - normed * mean_b)
        for c in range(blocks):
            gd_ref[c, r, EDGE : EDGE + cols, :] = gd[:, c * LANES : (c + 1) * LANES]
        fold = lambda v: jnp.sum(v.reshape(cols // 8, 8, chans), axis=0)
        return carry[0] + fold(gd), carry[1] + fold(prod), carry[2] + fold(gn)

    zero = jnp.zeros((8, chans), f32)
    sums = lax.fori_loop(0, rows, norm_step, (zero, zero, zero))
    for k in range(3):
        sums_ref[k : k + 1, :] = jnp.sum(sums[k], axis=0, keepdims=True)
    sums_ref[3:8, :] = jnp.zeros((5, chans), f32)

    def conv_step(c, carry):
        lanes = pl.ds(pl.multiple_of(c * LANES, LANES), LANES)
        for part in range(2):
            acc = conv_block(gd_ref, c, wexp, rows, part * half, half, True)
            for h in range(rows):
                span = slice(part * half, part * half + half)
                gi_ref[h, span, lanes] = (g_ref[h, span, lanes].astype(f32) + acc[h].reshape(half, LANES)).astype(bf16)
        return carry

    lax.fori_loop(0, blocks, conv_step, 0)


def tap_kernel(xp_ref, gd_ref, vecs_ref, sums_ref, *rest, taps, fast):
    *more, small_ref = rest
    blocks, rows, padded, _ = xp_ref.shape
    cols = padded - 2 * EDGE
    chans = blocks * LANES

    def step(c, carry):
        lanes = pl.ds(pl.multiple_of(c * LANES, LANES), LANES)
        for j in range(7):
            acc = [None] * 7
            for b in range(0, cols, 16):
                grads = [gd_ref[c, h, EDGE + b : EDGE + b + 16, :].reshape(2, 8, LANES) for h in range(rows)]
                for hp in range(rows):
                    at = EDGE + b + j - 3
                    piece = xp_ref[c, hp, at : at + 16, :].reshape(2, 8, LANES)
                    for h in range(max(0, hp - 3), min(rows, hp + 4)):
                        i = hp - h + 3
                        term = grads[h] * piece
                        term = term[0] + term[1]
                        acc[i] = term if acc[i] is None else acc[i] + term
            for i in range(7):
                small_ref[7 * i + j : 7 * i + j + 1, lanes] = jnp.sum(acc[i], axis=0, keepdims=True)
        return carry

    small_ref[taps:, :] = jnp.zeros((small_ref.shape[0] - taps, chans), f32)
    lax.fori_loop(0, blocks, step, 0)
    small_ref[taps : taps + 3, :] = sums_ref[0:3, :]
    small_ref[taps + 3 : taps + 4, :] = vecs_ref[3:4, :]
    if fast:
        scales, bsums = more[:4], more[4:]
        total = scales[0][...] + scales[1][...] + scales[2][...] + scales[3][...]
        row = jnp.sum(total, axis=0, keepdims=True) / vecs_ref[1:2, :] + vecs_ref[2:3, :] * vecs_ref[4:5, :]
        small_ref[taps + 4 : taps + 5, :] = row
        chip, _ = place()
        for k in range(4):
            small_ref[pl.ds(taps + 5 + lax.bitwise_xor(chip, k), 1), :] = bsums[k][0:1, :]


def merge_kernel(o1_ref, o2_ref, x_ref, y_ref, out1_ref, out2_ref, *, factor):
    part = o1_ref.shape[0]
    out1_ref[...] = (o1_ref[...] + x_ref[0:part, :].astype(f32) + y_ref[0:part, :].astype(f32)) * factor
    out2_ref[...] = ((o2_ref[...] + x_ref[part:, :].astype(f32) + y_ref[part:, :].astype(f32)) * factor).T


def shifted(block, axis, distance):
    devices = range(lax.axis_size(axis))
    route = [(i - distance, i) for i in devices if i - distance in devices]
    return lax.ppermute(block, axis, route)


def swap(value, bit, count):
    return lax.ppermute(value, "dp", [(i, i ^ bit) for i in range(count)])


def shards(
    block_input,
    grad_output,
    depth_weight,
    depth_bias,
    norm_gain,
    norm_shift,
    pw1_weight,
    pw1_bias,
    pw2_weight,
    pw2_bias,
    layer_scale,
):
    x, g = block_input[0, 0], grad_output[0, 0]
    rows, cols, chans = x.shape
    cells = rows * cols
    blocks = chans // LANES
    taps = depth_weight.shape[1]
    w1, w2 = pw1_weight[0], pw2_weight[0]
    units = w1.shape[0]
    replicas = lax.axis_size("dp")
    factor = 1.0 / replicas
    wide = 768
    part = wide // 2
    fast = replicas == 8 and units == 4 * wide

    wexp = struct((blocks, taps, 8, LANES), f32)
    padded = struct((blocks, rows, cols + 2 * EDGE, LANES), f32)
    like = lambda v: struct(v.shape, v.dtype)
    hbm = pl.BlockSpec(memory_space=pltpu.HBM)
    front_args = (x, g, depth_weight[0], depth_bias, norm_gain, norm_shift, layer_scale, pw2_bias, w1, pw1_bias, w2)
    acts, normed, rstd, xp, vecs, wexp, gv, w1, b1, w2 = call(
        front_kernel,
        (struct((2 * cells, chans), bf16), struct((cells, chans), f32), struct((cells, LANES), f32), padded, struct((8, chans), f32), wexp,
         like(g), like(w1), like(pw1_bias), like(w2)),
        *(pltpu.with_memory_space_constraint(v, pltpu.HBM) for v in front_args),
        name="front", in_specs=[hbm] * 11, cost=estimate(1e10, 1e6),
        scratch=[pltpu.VMEM(x.shape, bf16), pltpu.VMEM((taps, chans), bf16), pltpu.VMEM((8, chans), f32),
                 pltpu.SemaphoreType.DMA((11,))],
    )

    def wide_step(slot, gn):
        outs = (struct((cells, chans), f32), struct((8, wide), f32), struct((wide, cells), bf16),
                struct((wide, cells), bf16))
        first = gn is None
        args = (acts, w1, b1, w2) + (() if first else (gn,))
        return call(
            lambda *refs: wide_kernel(*refs, first=first, slot=slot), outs, *args,
            name="wide", aliases={} if first else {4: 0}, cost=estimate(1e10, 1e6),
        )

    def flip(k):
        return lambda chip: lax.bitwise_xor(chip, k)

    if fast:
        acts_s = swap(acts, 1, replicas)

        def share(k, keep, got, types):
            outs = (struct((part, chans), types), struct((part, chans), types), struct((8, chans), f32))
            return call(lambda *refs: share_kernel(*refs, slot=flip(k), mode="split"), outs,
                        w2, acts, acts_s, keep, got, name="share", cost=estimate(1e6, 1e3))

        def share_pack(k, keep, got, more, mode):
            outs = (struct((wide, chans), bf16), struct((8, chans), f32))
            return call(lambda *refs: share_kernel(*refs, slot=flip(k), mode=mode), outs,
                        w2, acts, acts_s, keep, got, more, name="pack", cost=estimate(1e10, 1e6))

        gn, bd, keep_d, send_d = wide_step(flip(3), None)
        got_d = swap(send_d, 1, replicas)
        gn, bx, keep_x, send_x = wide_step(flip(1), gn)
        got_x = swap(send_x, 1, replicas)
        d1, d2, sc_d = share(3, keep_d, got_d, bf16)
        gn, d1, d2 = lax.optimization_barrier((gn, d1, d2))
        d1_in, d2_in = swap(d1, 2, replicas), swap(d2, 4, replicas)
        gn, by, keep_y, send_y = wide_step(flip(2), gn)
        got_y = swap(send_y, 1, replicas)
        gn, bo, keep_o, send_o = wide_step(flip(0), gn)
        got_o = swap(send_o, 1, replicas)
        pack_x, sc_x = share_pack(1, keep_x, got_x, d2_in, "second")
        gn, pack_x, d1_in = lax.optimization_barrier((gn, pack_x, d1_in))
        pack_y, sc_y = share_pack(2, keep_y, got_y, d1_in, "first")
        gn, pack_y = lax.optimization_barrier((gn, pack_y))
        x_in, y_in = swap(pack_x, 2, replicas), swap(pack_y, 4, replicas)
    else:
        core = lax.axis_index("dp") % 2
        gn, bsums, g1, g2 = None, [], [], []
        for p in range(units // wide):
            gn, bsum, keep, send = wide_step(lambda chip, p=p: jnp.int32(p), gn)
            lo, hi = jnp.where(core == 0, keep, send), jnp.where(core == 0, send, keep)
            bsums.append(bsum[0:1])
            g1 += [dot(v[:part], acts[:cells]) for v in (lo, hi)]
            g2 += [dot(v[part:], acts[cells:]) for v in (lo, hi)]
        g1, g2 = jnp.concatenate(g1, axis=0), jnp.concatenate(g2, axis=0).T

    gi, gd, sums = call(
        back_kernel,
        (struct((rows, cols, chans), bf16), padded, struct((8, chans), f32)),
        gn, normed, rstd, vecs, gv, wexp,
        name="back", cost=estimate(1e6, 1e3),
    )
    received = shifted(gi, "section", -1)

    if fast:
        o1, o2, sc_o = share(0, keep_o, got_o, f32)
        more = (sc_d, sc_x, sc_y, sc_o, bo, bx, by, bd)
    else:
        more = ()
    total_rows = -(-(taps + 5 + units // chans) // 8) * 8
    small = call(lambda *refs: tap_kernel(*refs, taps=taps, fast=fast), struct((total_rows, chans), f32),
                 xp, gd, vecs, sums, *more, name="taps", cost=estimate(1e6, 1e3))

    if fast:
        small = jnp.sum(lax.all_gather(small.astype(bf16), "dp").astype(f32), axis=0)
        out1, out2 = call(
            lambda *refs: merge_kernel(*refs, factor=factor),
            (struct((part, chans), f32), struct((chans, part), f32)),
            o1, o2, x_in, y_in, name="merge", cost=estimate(1e10, 1e6),
        )
    else:
        scale_sum = jnp.sum(g2 * w2.astype(f32), axis=1)
        gscale = scale_sum / layer_scale[0] + pw2_bias[0] * vecs[4]
        small = jnp.concatenate([small[: taps + 4], gscale[None], *bsums], axis=0)
        small = lax.psum(small, "dp")
        out1 = lax.psum_scatter(g1, "dp", scatter_dimension=0, tiled=True) * factor
        out2 = lax.psum_scatter(g2, "dp", scatter_dimension=1, tiled=True) * factor
    small = small * factor
    return (
        out1[None],
        out2[None],
        small[taps + 5 : taps + 5 + units // chans].reshape(1, -1),
        small[None, : taps + 5],
        received[None, None],
    )


def solution(mesh):
    in_specs = (
        P("section", "dp", None, None, None),
        P("section", "dp", None, None, None),
        P("section", None, None),
        P("section", None),
        P("section", None),
        P("section", None),
        P("section", None, None),
        P("section", None),
        P("section", None, None),
        P("section", None),
        P("section", None),
    )
    out_specs = (
        P("section", "dp", None),
        P("section", None, "dp"),
        P("section", None),
        P("section", None, None),
        P("section", "dp", None, None, None),
    )
    return jax.shard_map(shards, mesh=mesh, in_specs=in_specs, out_specs=out_specs, check_vma=False)
```

```python
import jax
import jax.numpy as jnp
from jax import lax
from jax.experimental import pallas as pl
from jax.experimental.pallas import tpu as pltpu
from jax.sharding import PartitionSpec as P

root_half = 0.7071067811865476
inv_root_two_pi = 0.3989422804014327
f32 = jnp.float32
bf16 = jnp.bfloat16
LANES = 128
EDGE = 8
VMEM_LIMIT = 12 * 1024 * 1024


def struct(shape, dtype):
    return jax.ShapeDtypeStruct(shape, dtype)


def call(body, out_shape, *args, name, aliases=None, scratch=(), scalars=0, in_specs=None, cost=None):
    vmem = pl.BlockSpec(memory_space=pltpu.VMEM)
    smem = pl.BlockSpec(memory_space=pltpu.SMEM)
    specs = [smem] * scalars + [vmem] * (len(args) - scalars) if in_specs is None else in_specs
    return pl.pallas_call(
        body,
        out_shape=out_shape,
        in_specs=specs,
        out_specs=jax.tree.map(lambda _: vmem, out_shape),
        scratch_shapes=list(scratch),
        input_output_aliases=aliases or {},
        compiler_params=pltpu.CompilerParams(vmem_limit_bytes=VMEM_LIMIT),
        cost_estimate=cost,
        name=name,
    )(*args)


def estimate(flops, nbytes):
    return pl.CostEstimate(flops=int(flops), transcendentals=0, bytes_accessed=int(nbytes))


def dot(a, b):
    return jnp.dot(a, b, preferred_element_type=f32)


def dot_last(a, b):
    return lax.dot_general(a, b, (((1,), (1,)), ((), ())), preferred_element_type=f32)


def place():
    me = lax.axis_index("dp")
    return lax.shift_right_logical(me, 1), lax.bitwise_and(me, 1)


def expand_taps(w_ref, wexp, blocks):
    for c in range(blocks):
        for k in range(w_ref.shape[0]):
            row = w_ref[k : k + 1, c * LANES : (c + 1) * LANES].astype(f32)
            wexp[c, k] = jnp.broadcast_to(row, (8, LANES))


def zero_edges(buf, blocks, rows, cols):
    zero = jnp.zeros((rows, EDGE, LANES), f32)
    for c in range(blocks):
        buf[c, :, 0:EDGE, :] = zero
        buf[c, :, EDGE + cols : EDGE + cols + EDGE, :] = zero


def conv_block(src, c, wexp, rows, start, width, flip):
    groups = width // 8
    acc = [None] * rows
    for j in range(7):
        at = start + EDGE + (3 - j if flip else j - 3)
        for hp in range(rows):
            piece = src[c, hp, at : at + width, :].reshape(groups, 8, LANES)
            for h in range(max(0, hp - 3), min(rows, hp + 4)):
                i = h - hp + 3 if flip else hp - h + 3
                term = piece * wexp[c, 7 * i + j]
                acc[h] = term if acc[h] is None else acc[h] + term
    return acc


def front_kernel(x_hbm, g_hbm, w_hbm, db_hbm, gain_hbm, shift_hbm, scale_hbm, bb_hbm, w1_hbm, b1_hbm, w2_hbm,
                 acts_ref, normed_ref, rstd_ref, xp_ref, vecs_ref, wexp, g_ref, w1_ref, b1_ref, w2_ref,
                 x_ref, w_ref, tmp_ref, sems):
    rows, cols, chans = x_ref.shape
    blocks = chans // LANES
    half = cols // 2
    moves = [(x_hbm, x_ref), (w_hbm, w_ref), (g_hbm, g_ref), (db_hbm, tmp_ref.at[0:1]), (gain_hbm, tmp_ref.at[1:2]),
             (shift_hbm, tmp_ref.at[2:3]), (scale_hbm, tmp_ref.at[3:4]), (bb_hbm, tmp_ref.at[4:5]),
             (w1_hbm, w1_ref), (b1_hbm, b1_ref), (w2_hbm, w2_ref)]
    copies = [pltpu.make_async_copy(src, dst, sems.at[k]) for k, (src, dst) in enumerate(moves)]
    for copy in copies:
        copy.start()
    zero_edges(xp_ref, blocks, rows, cols)
    copies[0].wait()
    for c in range(blocks):
        xp_ref[c, :, EDGE : EDGE + cols, :] = x_ref[:, :, c * LANES : (c + 1) * LANES].astype(f32)
    copies[1].wait()
    expand_taps(w_ref, wexp, blocks)

    def conv_step(c, carry):
        lanes = pl.ds(pl.multiple_of(c * LANES, LANES), LANES)
        for part in range(2):
            acc = conv_block(xp_ref, c, wexp, rows, part * half, half, False)
            for h in range(rows):
                normed_ref[h * cols + part * half : h * cols + part * half + half, lanes] = acc[h].reshape(half, LANES)
        return carry

    lax.fori_loop(0, blocks, conv_step, 0)
    for copy in copies[2:8]:
        copy.wait()
    bias, gain, shift, scale = (tmp_ref[k : k + 1, :] for k in range(4))

    def norm_step(r, carry):
        at = pl.ds(pl.multiple_of(r * cols, cols), cols)
        d = normed_ref[at, :] + bias
        d = d - jnp.mean(d, axis=-1, keepdims=True)
        rs = lax.rsqrt(jnp.mean(d * d, axis=-1, keepdims=True) + 1e-06)
        normed = d * rs
        normed_ref[at, :] = normed
        rstd_ref[at, :] = jnp.broadcast_to(rs, (cols, LANES))
        acts_ref[at, :] = (normed * gain + shift).astype(bf16)
        g = g_ref[r].astype(f32)
        gp = (g * scale).astype(bf16)
        acts_ref[pl.ds(pl.multiple_of((rows + r) * cols, cols), cols), :] = gp
        b2 = jnp.sum(gp.astype(f32).reshape(cols // 8, 8, chans), axis=0)
        gs = jnp.sum(g.reshape(cols // 8, 8, chans), axis=0)
        return carry[0] + b2, carry[1] + gs

    zero = jnp.zeros((8, chans), f32)
    b2, gs = lax.fori_loop(0, rows, norm_step, (zero, zero))
    vecs_ref[0:1, :] = gain
    vecs_ref[1:2, :] = scale
    vecs_ref[2:3, :] = tmp_ref[4:5, :]
    vecs_ref[3:4, :] = jnp.sum(b2, axis=0, keepdims=True)
    vecs_ref[4:5, :] = jnp.sum(gs, axis=0, keepdims=True)
    vecs_ref[5:8, :] = jnp.zeros((3, chans), f32)
    for copy in copies[8:]:
        copy.wait()


def wide_kernel(acts_ref, w1_ref, b1_ref, w2_ref, *rest, first, slot):
    *gin, gn_ref, bsum_ref, keep_ref, send_ref = rest
    cells = acts_ref.shape[0] // 2
    wide = bsum_ref.shape[1]
    part = wide // 2
    chip, core = place()
    at = pl.multiple_of(slot(chip) * wide, wide)
    w1 = w1_ref[pl.ds(at, wide), :]
    w2 = w2_ref[:, pl.ds(at, wide)]
    b1 = b1_ref[:, pl.ds(at, wide)]
    pre = dot_last(acts_ref[0:cells, :], w1) + b1
    cdf = 0.5 * (1.0 + lax.erf(pre * root_half))
    hidden = (pre * cdf).astype(bf16)
    ghid = dot(acts_ref[cells:, :], w2)
    density = jnp.exp(-0.5 * pre * pre) * inv_root_two_pi
    gpre = (ghid * (cdf + pre * density)).astype(bf16)
    total = jnp.sum(gpre.astype(f32), axis=0, keepdims=True)
    bsum_ref[...] = jnp.broadcast_to(total, (8, wide))
    gn = dot(gpre, w1)
    gn_ref[...] = gn if first else gin[0][...] + gn
    gt, ht = gpre.T, hidden.T
    for side in range(2):
        @pl.when(core == side)
        def _(side=side):
            k, s = side * part, (1 - side) * part
            keep_ref[0:part, :] = gt[k : k + part, :]
            send_ref[0:part, :] = gt[s : s + part, :]
            keep_ref[part:, :] = ht[k : k + part, :]
            send_ref[part:, :] = ht[s : s + part, :]


def share_kernel(w2_ref, own_ref, sib_ref, keep_ref, got_ref, d1_ref, d2_ref, scale_ref, *, slot):
    part = keep_ref.shape[0] // 2
    cells = own_ref.shape[0] // 2
    chip, core = place()
    at = pl.multiple_of((2 * slot(chip) + core) * part, part)
    d1 = dot(keep_ref[0:part, :], own_ref[0:cells, :]) + dot(got_ref[0:part, :], sib_ref[0:cells, :])
    d1_ref[...] = d1.astype(d1_ref.dtype)
    d2 = dot(keep_ref[part:, :], own_ref[cells:, :]) + dot(got_ref[part:, :], sib_ref[cells:, :])
    d2_ref[...] = d2.astype(d2_ref.dtype)
    prod = d2 * w2_ref[:, pl.ds(at, part)].T.astype(f32)
    scale_ref[...] = jnp.sum(prod.reshape(part // 8, 8, prod.shape[1]), axis=0)


def relay_kernel(direct_ref, base_ref, more_ref, pack_ref):
    part = direct_ref.shape[0]
    pack_ref[0:part, :] = direct_ref[...]
    pack_ref[part:, :] = (base_ref[...] + more_ref[...].astype(f32)).astype(bf16)


def back_kernel(gn_ref, normed_ref, rstd_ref, vecs_ref, g_ref, wexp, gi_ref, gd_ref, sums_ref):
    rows, cols, chans = g_ref.shape
    blocks = chans // LANES
    half = cols // 2
    zero_edges(gd_ref, blocks, rows, cols)
    gain = vecs_ref[0:1, :]

    def norm_step(r, carry):
        at = pl.ds(pl.multiple_of(r * cols, cols), cols)
        gn = gn_ref[at, :]
        normed = normed_ref[at, :]
        prod = gn * normed
        scaled = gn * gain
        mean_a = jnp.mean(scaled, axis=-1, keepdims=True)
        mean_b = jnp.mean(prod * gain, axis=-1, keepdims=True)
        rs = rstd_ref[at, 0:1]
        gd = rs * (scaled - mean_a - normed * mean_b)
        for c in range(blocks):
            gd_ref[c, r, EDGE : EDGE + cols, :] = gd[:, c * LANES : (c + 1) * LANES]
        fold = lambda v: jnp.sum(v.reshape(cols // 8, 8, chans), axis=0)
        return carry[0] + fold(gd), carry[1] + fold(prod), carry[2] + fold(gn)

    zero = jnp.zeros((8, chans), f32)
    sums = lax.fori_loop(0, rows, norm_step, (zero, zero, zero))
    for k in range(3):
        sums_ref[k : k + 1, :] = jnp.sum(sums[k], axis=0, keepdims=True)
    sums_ref[3:8, :] = jnp.zeros((5, chans), f32)

    def conv_step(c, carry):
        lanes = pl.ds(pl.multiple_of(c * LANES, LANES), LANES)
        for part in range(2):
            acc = conv_block(gd_ref, c, wexp, rows, part * half, half, True)
            for h in range(rows):
                span = slice(part * half, part * half + half)
                gi_ref[h, span, lanes] = (g_ref[h, span, lanes].astype(f32) + acc[h].reshape(half, LANES)).astype(bf16)
        return carry

    lax.fori_loop(0, blocks, conv_step, 0)


def tap_kernel(xp_ref, gd_ref, vecs_ref, sums_ref, *rest, taps, fast):
    *more, small_ref = rest
    blocks, rows, padded, _ = xp_ref.shape
    cols = padded - 2 * EDGE
    chans = blocks * LANES

    def step(c, carry):
        lanes = pl.ds(pl.multiple_of(c * LANES, LANES), LANES)
        for j in range(7):
            acc = [None] * 7
            for b in range(0, cols, 16):
                grads = [gd_ref[c, h, EDGE + b : EDGE + b + 16, :].reshape(2, 8, LANES) for h in range(rows)]
                for hp in range(rows):
                    at = EDGE + b + j - 3
                    piece = xp_ref[c, hp, at : at + 16, :].reshape(2, 8, LANES)
                    for h in range(max(0, hp - 3), min(rows, hp + 4)):
                        i = hp - h + 3
                        term = grads[h] * piece
                        term = term[0] + term[1]
                        acc[i] = term if acc[i] is None else acc[i] + term
            for i in range(7):
                small_ref[7 * i + j : 7 * i + j + 1, lanes] = jnp.sum(acc[i], axis=0, keepdims=True)
        return carry

    small_ref[taps:, :] = jnp.zeros((small_ref.shape[0] - taps, chans), f32)
    lax.fori_loop(0, blocks, step, 0)
    small_ref[taps : taps + 3, :] = sums_ref[0:3, :]
    small_ref[taps + 3 : taps + 4, :] = vecs_ref[3:4, :]
    if fast:
        scales, bsums = more[:4], more[4:]
        total = scales[0][...] + scales[1][...] + scales[2][...] + scales[3][...]
        row = jnp.sum(total, axis=0, keepdims=True) / vecs_ref[1:2, :] + vecs_ref[2:3, :] * vecs_ref[4:5, :]
        small_ref[taps + 4 : taps + 5, :] = row
        chip, _ = place()
        for k in range(4):
            small_ref[pl.ds(taps + 5 + lax.bitwise_xor(chip, k), 1), :] = bsums[k][0:1, :]


def merge_kernel(o1_ref, o2_ref, x_ref, y_ref, all_ref, gi_ref,
                 out1_ref, out2_ref, bias_ref, small_ref, recv_hbm, stage_ref, sem, *, factor):
    part, chans = o1_ref.shape
    move = pltpu.make_async_copy(gi_ref, recv_hbm, sem)
    move.start()
    out1_ref[...] = (o1_ref[...] + x_ref[0:part, :].astype(f32) + y_ref[part:, :].astype(f32)) * factor
    out2_ref[...] = ((o2_ref[...] + x_ref[part:, :].astype(f32) + y_ref[0:part, :].astype(f32)) * factor).T
    total = all_ref[0].astype(f32)
    for k in range(1, all_ref.shape[0]):
        total = total + all_ref[k].astype(f32)
    total = total * factor
    rows = small_ref.shape[0]
    stage_ref[...] = total
    for k in range(rows):
        small_ref[k] = stage_ref[k : k + 1, :]
    for k in range(bias_ref.shape[1] // chans):
        bias_ref[:, k * chans : (k + 1) * chans] = stage_ref[rows + k : rows + k + 1, :]
    move.wait()


def shifted(block, axis, distance):
    devices = range(lax.axis_size(axis))
    route = [(i - distance, i) for i in devices if i - distance in devices]
    return lax.ppermute(block, axis, route)


def swap(value, bit, count):
    return lax.ppermute(value, "dp", [(i, i ^ bit) for i in range(count)])


def shards(
    block_input,
    grad_output,
    depth_weight,
    depth_bias,
    norm_gain,
    norm_shift,
    pw1_weight,
    pw1_bias,
    pw2_weight,
    pw2_bias,
    layer_scale,
):
    x, g = block_input[0, 0], grad_output[0, 0]
    rows, cols, chans = x.shape
    cells = rows * cols
    blocks = chans // LANES
    taps = depth_weight.shape[1]
    w1, w2 = pw1_weight[0], pw2_weight[0]
    units = w1.shape[0]
    replicas = lax.axis_size("dp")
    factor = 1.0 / replicas
    wide = 768
    part = wide // 2
    fast = replicas == 8 and units == 4 * wide

    wexp = struct((blocks, taps, 8, LANES), f32)
    padded = struct((blocks, rows, cols + 2 * EDGE, LANES), f32)
    like = lambda v: struct(v.shape, v.dtype)
    hbm = pl.BlockSpec(memory_space=pltpu.HBM)
    front_args = (x, g, depth_weight[0], depth_bias, norm_gain, norm_shift, layer_scale, pw2_bias, w1, pw1_bias, w2)
    acts, normed, rstd, xp, vecs, wexp, gv, w1, b1, w2 = call(
        front_kernel,
        (struct((2 * cells, chans), bf16), struct((cells, chans), f32), struct((cells, LANES), f32), padded, struct((8, chans), f32), wexp,
         like(g), like(w1), like(pw1_bias), like(w2)),
        *(pltpu.with_memory_space_constraint(v, pltpu.HBM) for v in front_args),
        name="front", in_specs=[hbm] * 11, cost=estimate(1e10, 1e6),
        scratch=[pltpu.VMEM(x.shape, bf16), pltpu.VMEM((taps, chans), bf16), pltpu.VMEM((8, chans), f32),
                 pltpu.SemaphoreType.DMA((11,))],
    )

    def wide_step(slot, gn):
        outs = (struct((cells, chans), f32), struct((8, wide), f32), struct((wide, cells), bf16),
                struct((wide, cells), bf16))
        first = gn is None
        args = (acts, w1, b1, w2) + (() if first else (gn,))
        return call(
            lambda *refs: wide_kernel(*refs, first=first, slot=slot), outs, *args,
            name="wide", aliases={} if first else {4: 0}, cost=estimate(1e10, 1e6),
        )

    def flip(k):
        return lambda chip: lax.bitwise_xor(chip, k)

    if fast:
        acts_s = swap(acts, 1, replicas)

        def share(k, keep, got, types):
            outs = (struct((part, chans), types[0]), struct((part, chans), types[1]), struct((8, chans), f32))
            return call(lambda *refs: share_kernel(*refs, slot=flip(k)), outs,
                        w2, acts, acts_s, keep, got, name="share", cost=estimate(1e6, 1e3))

        gn, bd, keep_d, send_d = wide_step(flip(3), None)
        got_d = swap(send_d, 1, replicas)
        d1, d2, sc_d = share(3, keep_d, got_d, (bf16, bf16))
        gn, d1, d2 = lax.optimization_barrier((gn, d1, d2))
        d1_in, d2_in = swap(d1, 2, replicas), swap(d2, 4, replicas)
        gn, bx, keep_x, send_x = wide_step(flip(1), gn)
        got_x = swap(send_x, 1, replicas)
        gn, by, keep_y, send_y = wide_step(flip(2), gn)
        got_y = swap(send_y, 1, replicas)
        gn, bo, keep_o, send_o = wide_step(flip(0), gn)
        got_o = swap(send_o, 1, replicas)
        gn, got_x = lax.optimization_barrier((gn, got_x))
        x1, x2, sc_x = share(1, keep_x, got_x, (bf16, f32))
        x1, got_y = lax.optimization_barrier((x1, got_y))
        y1, y2, sc_y = share(2, keep_y, got_y, (f32, bf16))
        x1, x2, y1, y2, d1_in, d2_in = lax.optimization_barrier((x1, x2, y1, y2, d1_in, d2_in))

        def relay(direct, base, more):
            return call(relay_kernel, struct((wide, chans), bf16), direct, base, more,
                        name="relay", cost=estimate(1e6, 1e3))

        pack_x = relay(x1, x2, d2_in)
        y2, pack_x = lax.optimization_barrier((y2, pack_x))
        pack_y = relay(y2, y1, d1_in)
        gn, pack_y = lax.optimization_barrier((gn, pack_y))
        x_in, y_in = swap(pack_x, 2, replicas), swap(pack_y, 4, replicas)
    else:
        core = lax.axis_index("dp") % 2
        gn, bsums, g1, g2 = None, [], [], []
        for p in range(units // wide):
            gn, bsum, keep, send = wide_step(lambda chip, p=p: jnp.int32(p), gn)
            lo, hi = jnp.where(core == 0, keep, send), jnp.where(core == 0, send, keep)
            bsums.append(bsum[0:1])
            g1 += [dot(v[:part], acts[:cells]) for v in (lo, hi)]
            g2 += [dot(v[part:], acts[cells:]) for v in (lo, hi)]
        g1, g2 = jnp.concatenate(g1, axis=0), jnp.concatenate(g2, axis=0).T

    gi, gd, sums = call(
        back_kernel,
        (struct((rows, cols, chans), bf16), padded, struct((8, chans), f32)),
        gn, normed, rstd, vecs, gv, wexp,
        name="back", cost=estimate(1e6, 1e3),
    )
    if fast:
        gi, got_o = lax.optimization_barrier((gi, got_o))
    received = shifted(gi, "section", -1)

    if fast:
        o1, o2, sc_o = share(0, keep_o, got_o, (f32, f32))
        more = (sc_d, sc_x, sc_y, sc_o, bo, bx, by, bd)
    else:
        more = ()
    total_rows = -(-(taps + 5 + units // chans) // 8) * 8
    small = call(lambda *refs: tap_kernel(*refs, taps=taps, fast=fast), struct((total_rows, chans), f32),
                 xp, gd, vecs, sums, *more, name="taps", cost=estimate(1e6, 1e3))

    if fast:
        every = lax.all_gather(small.astype(bf16), "dp")
        vmem = pl.BlockSpec(memory_space=pltpu.VMEM)
        out1, out2, bias, small, received = pl.pallas_call(
            lambda *refs: merge_kernel(*refs, factor=factor),
            out_shape=(struct((part, chans), f32), struct((chans, part), f32), struct((1, units), f32),
                       struct((taps + 5, 1, chans), f32), like(gi)),
            in_specs=[vmem] * 6,
            out_specs=(vmem,) * 4 + (pl.BlockSpec(memory_space=pltpu.HBM),),
            scratch_shapes=[pltpu.VMEM((total_rows, chans), f32), pltpu.SemaphoreType.DMA],
            compiler_params=pltpu.CompilerParams(vmem_limit_bytes=VMEM_LIMIT),
            name="merge",
        )(o1, o2, x_in, y_in, every, received)
        small = jnp.transpose(small, (1, 0, 2))
    else:
        scale_sum = jnp.sum(g2 * w2.astype(f32), axis=1)
        gscale = scale_sum / layer_scale[0] + pw2_bias[0] * vecs[4]
        small = jnp.concatenate([small[: taps + 4], gscale[None], *bsums], axis=0)
        small = lax.psum(small, "dp")
        out1 = lax.psum_scatter(g1, "dp", scatter_dimension=0, tiled=True) * factor
        out2 = lax.psum_scatter(g2, "dp", scatter_dimension=1, tiled=True) * factor
        small = small * factor
        bias, small = small[taps + 5 :].reshape(1, -1), small[None, : taps + 5]
    return (out1[None], out2[None], bias, small, received[None, None])


def solution(mesh):
    in_specs = (
        P("section", "dp", None, None, None),
        P("section", "dp", None, None, None),
        P("section", None, None),
        P("section", None),
        P("section", None),
        P("section", None),
        P("section", None, None),
        P("section", None),
        P("section", None, None),
        P("section", None),
        P("section", None),
    )
    out_specs = (
        P("section", "dp", None),
        P("section", None, "dp"),
        P("section", None),
        P("section", None, None),
        P("section", "dp", None, None, None),
    )
    return jax.shard_map(shards, mesh=mesh, in_specs=in_specs, out_specs=out_specs, check_vma=False)
```

```python
import jax
import jax.numpy as jnp
from jax import lax
from jax.experimental import pallas as pl
from jax.experimental.pallas import tpu as pltpu
from jax.sharding import PartitionSpec as P

root_half = 0.7071067811865476
inv_root_two_pi = 0.3989422804014327
f32 = jnp.float32
bf16 = jnp.bfloat16
LANES = 128
EDGE = 8
VMEM_LIMIT = 12 * 1024 * 1024


def struct(shape, dtype):
    return jax.ShapeDtypeStruct(shape, dtype)


def call(body, out_shape, *args, name, aliases=None, scratch=(), scalars=0, in_specs=None, cost=None):
    vmem = pl.BlockSpec(memory_space=pltpu.VMEM)
    smem = pl.BlockSpec(memory_space=pltpu.SMEM)
    specs = [smem] * scalars + [vmem] * (len(args) - scalars) if in_specs is None else in_specs
    return pl.pallas_call(
        body,
        out_shape=out_shape,
        in_specs=specs,
        out_specs=jax.tree.map(lambda _: vmem, out_shape),
        scratch_shapes=list(scratch),
        input_output_aliases=aliases or {},
        compiler_params=pltpu.CompilerParams(vmem_limit_bytes=VMEM_LIMIT),
        cost_estimate=cost,
        name=name,
    )(*args)


def estimate(flops, nbytes):
    return pl.CostEstimate(flops=int(flops), transcendentals=0, bytes_accessed=int(nbytes))


def dot(a, b):
    return jnp.dot(a, b, preferred_element_type=f32)


def dot_last(a, b):
    return lax.dot_general(a, b, (((1,), (1,)), ((), ())), preferred_element_type=f32)


def place():
    me = lax.axis_index("dp")
    return lax.shift_right_logical(me, 1), lax.bitwise_and(me, 1)


def expand_taps(w_ref, wexp, blocks):
    count = w_ref.shape[0]
    for c in range(blocks):
        rows = [w_ref[k : k + 1, c * LANES : (c + 1) * LANES].astype(f32) for k in range(count)]
        for k in range(count):
            wexp[c, k] = jnp.broadcast_to(rows[k], (8, LANES))
        for i in range(6):
            for j in range(7):
                wexp[c, count + 7 * i + j] = jnp.broadcast_to(rows[7 * i + j] + rows[7 * i + 7 + j], (8, LANES))


def zero_edges(buf, blocks, rows, cols):
    zero = jnp.zeros((rows, EDGE, LANES), f32)
    for c in range(blocks):
        buf[c, :, 0:EDGE, :] = zero
        buf[c, :, EDGE + cols : EDGE + cols + EDGE, :] = zero


def conv_block(src, c, wexp, rows, start, width, flip):
    groups = width // 8
    pairs = rows // 2
    tap = lambda k: 3 - k if flip else k + 3
    lone = lambda k, j: wexp[c, 7 * tap(k) + j]
    both = lambda k, j: wexp[c, 49 + 7 * min(tap(k), tap(k + 1)) + j]
    odd, even, mixed = [None] * pairs, [None] * (pairs + 1), [None] * pairs

    def put(acc, a, term):
        acc[a] = term if acc[a] is None else acc[a] + term

    for j in range(7):
        at = start + EDGE + (3 - j if flip else j - 3)
        for b in range(pairs):
            x0, x1 = (src[c, 2 * b + k, at : at + width, :].reshape(groups, 8, LANES) for k in range(2))
            for d in range(-1, 2):
                if 0 <= b - d < pairs:
                    put(odd, b - d, x1 * lone(2 * d, j))
            for d in range(-2, 2):
                if 0 <= b - d <= pairs:
                    put(even, b - d, x0 * lone(2 * d + 1, j))
            x0 = x0 + x1
            for d in range(-2, 2):
                if 0 <= b - d < pairs:
                    put(mixed, b - d, x0 * (lone(-3, j) if d == -2 else both(2 * d, j)))
    acc = []
    for a in range(pairs):
        acc += [mixed[a] - odd[a] - even[a], odd[a] + even[a + 1]]
    return acc


def load_kernel(x_hbm, g_hbm, w_hbm, db_hbm, gain_hbm, shift_hbm, scale_hbm, bb_hbm,
                gp_ref, xp_ref, vecs_ref, wexp, g_ref, tmp_ref, x_ref, w_ref, sems):
    rows, cols, chans = x_ref.shape
    blocks = chans // LANES
    moves = [(w_hbm, w_ref), (scale_hbm, tmp_ref.at[3:4]), (g_hbm, g_ref), (x_hbm, x_ref), (db_hbm, tmp_ref.at[0:1]),
             (gain_hbm, tmp_ref.at[1:2]), (shift_hbm, tmp_ref.at[2:3]), (bb_hbm, tmp_ref.at[4:5])]
    copies = [pltpu.make_async_copy(src, dst, sems.at[k]) for k, (src, dst) in enumerate(moves)]
    for copy in copies:
        copy.start()
    zero_edges(xp_ref, blocks, rows, cols)
    copies[0].wait()
    expand_taps(w_ref, wexp, blocks)
    copies[1].wait()
    copies[2].wait()
    b2, gs = [], []
    for c in range(blocks):
        lanes = slice(c * LANES, (c + 1) * LANES)
        g = g_ref[:, :, lanes].astype(f32).reshape(rows * cols, LANES)
        gp = (g * tmp_ref[3:4, lanes]).astype(bf16)
        gp_ref[:, lanes] = gp
        b2.append(jnp.sum(gp.astype(f32), axis=0, keepdims=True))
        gs.append(jnp.sum(g, axis=0, keepdims=True))
    copies[3].wait()
    for c in range(blocks):
        xp_ref[c, :, EDGE : EDGE + cols, :] = x_ref[:, :, c * LANES : (c + 1) * LANES].astype(f32)
    for copy in copies[4:]:
        copy.wait()
    vecs_ref[0:1, :] = tmp_ref[1:2, :]
    vecs_ref[1:2, :] = tmp_ref[3:4, :]
    vecs_ref[2:3, :] = tmp_ref[4:5, :]
    vecs_ref[3:4, :] = jnp.concatenate(b2, axis=1)
    vecs_ref[4:5, :] = jnp.concatenate(gs, axis=1)
    vecs_ref[5:8, :] = jnp.zeros((3, chans), f32)


def front_kernel(xp_ref, wexp, tmp_ref, w1_hbm, b1_hbm, w2_hbm,
                 yn_ref, normed_ref, rstd_ref, w1_ref, b1_ref, w2_ref, mean_ref, sems):
    blocks, rows, padded, _ = xp_ref.shape
    cols = padded - 2 * EDGE
    chans = blocks * LANES
    half = cols // 4
    moves = [(w1_hbm, w1_ref), (b1_hbm, b1_ref), (w2_hbm, w2_ref)]
    copies = [pltpu.make_async_copy(src, dst, sems.at[k]) for k, (src, dst) in enumerate(moves)]
    for copy in copies:
        copy.start()
    mean_ref[...] = jnp.zeros(mean_ref.shape, f32)

    def conv_step(c, carry):
        lanes = pl.ds(pl.multiple_of(c * LANES, LANES), LANES)
        for part in range(4):
            acc = conv_block(xp_ref, c, wexp, rows, part * half, half, False)
            bias = tmp_ref[0:1, lanes]
            for h in range(rows):
                at = slice(h * cols + part * half, h * cols + part * half + half)
                value = acc[h].reshape(half, LANES) + bias
                normed_ref[at, lanes] = value
                mean_ref[at, :] = mean_ref[at, :] + value
        return carry

    lax.fori_loop(0, blocks, conv_step, 0)
    mean_ref[...] = jnp.broadcast_to(jnp.sum(mean_ref[...], axis=-1, keepdims=True) * (1.0 / chans), mean_ref.shape)

    def spread_step(r, carry):
        at = pl.ds(pl.multiple_of(r * cols, cols), cols)
        mean = mean_ref[at, :]
        total = jnp.zeros((cols, LANES), f32)
        for c in range(blocks):
            d = normed_ref[at, c * LANES : (c + 1) * LANES] - mean
            total = total + d * d
        rstd_ref[at, :] = total
        return carry

    lax.fori_loop(0, rows, spread_step, 0)
    var = jnp.sum(rstd_ref[...], axis=-1, keepdims=True) * (1.0 / chans)
    rstd_ref[...] = jnp.broadcast_to(lax.rsqrt(var + 1e-06), rstd_ref.shape)
    gain, shift = tmp_ref[1:2, :], tmp_ref[2:3, :]

    def norm_step(r, carry):
        at = pl.ds(pl.multiple_of(r * cols, cols), cols)
        mean, rs = mean_ref[at, :], rstd_ref[at, :]
        for c in range(blocks):
            lanes = slice(c * LANES, (c + 1) * LANES)
            normed = (normed_ref[at, lanes] - mean) * rs
            normed_ref[at, lanes] = normed
            yn_ref[at, lanes] = (normed * gain[:, lanes] + shift[:, lanes]).astype(bf16)
        return carry

    lax.fori_loop(0, rows, norm_step, 0)
    for copy in copies:
        copy.wait()


def gate(pre):
    return 0.5 * (1.0 + lax.erf(pre * root_half))


def split_store(core, part, value, keep_ref, send_ref, row):
    for side in range(2):
        @pl.when(core == side)
        def _(side=side):
            k, s = side * part, (1 - side) * part
            keep_ref[row : row + part, :] = value[k : k + part, :]
            send_ref[row : row + part, :] = value[s : s + part, :]


def slope_of(pre, cdf):
    density = jnp.exp(-0.5 * pre * pre) * inv_root_two_pi
    return cdf + pre * density


def open_kernel(yn_ref, w1_ref, b1_ref, rise_ref, keep_ref, send_ref, *, slot):
    wide = rise_ref.shape[1]
    chip, core = place()
    at = pl.multiple_of(slot(chip) * wide, wide)
    pre = dot_last(yn_ref[...], w1_ref[pl.ds(at, wide), :]) + b1_ref[:, pl.ds(at, wide)]
    cdf = gate(pre)
    rise_ref[...] = slope_of(pre, cdf)
    split_store(core, wide // 2, (pre * cdf).astype(bf16).T, keep_ref, send_ref, 0)


def close_kernel(gp_ref, rise_ref, w2_ref, gpre_ref, keep_ref, send_ref, *, slot):
    wide = rise_ref.shape[1]
    chip, core = place()
    at = pl.multiple_of(slot(chip) * wide, wide)
    gpre = (dot(gp_ref[...], w2_ref[:, pl.ds(at, wide)]) * rise_ref[...]).astype(bf16)
    gpre_ref[...] = gpre
    split_store(core, wide // 2, gpre.T, keep_ref, send_ref, 0)


def wide_kernel(yn_ref, gp_ref, w1_ref, b1_ref, w2_ref, *rest, mode, slot, other):
    *more, bsum_ref, keep_ref, send_ref = rest
    wide = bsum_ref.shape[1]
    part = wide // 2
    chip, core = place()
    at = pl.multiple_of(slot(chip) * wide, wide)
    w1 = w1_ref[pl.ds(at, wide), :]
    w2 = w2_ref[:, pl.ds(at, wide)]
    pre = dot_last(yn_ref[...], w1) + b1_ref[:, pl.ds(at, wide)]
    cdf = gate(pre)
    hidden = (pre * cdf).astype(bf16)
    gpre = (dot(gp_ref[...], w2) * slope_of(pre, cdf)).astype(bf16)
    bsum_ref[...] = jnp.broadcast_to(jnp.sum(gpre.astype(f32), axis=0, keepdims=True), (8, wide))
    gn = dot(gpre, w1)
    if mode == "first":
        (gn_ref,) = more
        gn_ref[...] = gn
    elif mode == "next":
        gin_ref, gn_ref = more
        gn_ref[...] = gin_ref[...] + gn
    else:
        gpre_ref, gn_ref, osum_ref = more
        back = pl.multiple_of(other(chip) * wide, wide)
        gn_ref[...] = gn + dot(gpre_ref[...], w1_ref[pl.ds(back, wide), :])
        total = jnp.sum(gpre_ref[...].astype(f32), axis=0, keepdims=True)
        osum_ref[...] = jnp.broadcast_to(total, (8, wide))
    split_store(core, part, gpre.T, keep_ref, send_ref, 0)
    split_store(core, part, hidden.T, keep_ref, send_ref, part)


def half_kernel(own_ref, sib_ref, keep_ref, got_ref, *rest, slot):
    if slot is None:
        (d_ref,) = rest
    else:
        w2_ref, d_ref, scale_ref = rest
    d = dot(keep_ref[...], own_ref[...]) + dot(got_ref[...], sib_ref[...])
    d_ref[...] = d.astype(d_ref.dtype)
    if slot is not None:
        part, chans = d.shape
        chip, core = place()
        at = pl.multiple_of((2 * slot(chip) + core) * part, part)
        prod = d * w2_ref[:, pl.ds(at, part)].T.astype(f32)
        scale_ref[...] = jnp.sum(prod.reshape(part // 8, 8, chans), axis=0)


def share_kernel(w2_ref, yo_ref, ys_ref, go_ref, gs_ref, keep_ref, got_ref, d1_ref, d2_ref, scale_ref, *, slot):
    part = keep_ref.shape[0] // 2
    first, second = slice(0, part), slice(part, 2 * part)
    half_kernel(yo_ref, ys_ref, keep_ref.at[first, :], got_ref.at[first, :], d1_ref, slot=None)
    half_kernel(go_ref, gs_ref, keep_ref.at[second, :], got_ref.at[second, :], w2_ref, d2_ref, scale_ref, slot=slot)


def relay_kernel(direct_ref, base_ref, more_ref, pack_ref):
    part = direct_ref.shape[0]
    pack_ref[0:part, :] = direct_ref[...]
    pack_ref[part:, :] = (base_ref[...] + more_ref[...].astype(f32)).astype(bf16)


def slope_kernel(gn_ref, normed_ref, rstd_ref, vecs_ref, gd_ref, sums_ref):
    blocks, rows, padded, _ = gd_ref.shape
    cols = padded - 2 * EDGE
    chans = blocks * LANES
    zero_edges(gd_ref, blocks, rows, cols)
    gain = vecs_ref[0:1, :]

    def norm_step(r, carry):
        at = pl.ds(pl.multiple_of(r * cols, cols), cols)
        gn = gn_ref[at, :]
        normed = normed_ref[at, :]
        prod = gn * normed
        scaled = gn * gain
        mean_a = jnp.mean(scaled, axis=-1, keepdims=True)
        mean_b = jnp.mean(prod * gain, axis=-1, keepdims=True)
        rs = rstd_ref[at, 0:1]
        gd = rs * (scaled - mean_a - normed * mean_b)
        for c in range(blocks):
            gd_ref[c, r, EDGE : EDGE + cols, :] = gd[:, c * LANES : (c + 1) * LANES]
        fold = lambda v: jnp.sum(v.reshape(cols // 8, 8, chans), axis=0)
        return carry[0] + fold(gd), carry[1] + fold(prod), carry[2] + fold(gn)

    zero = jnp.zeros((8, chans), f32)
    sums = lax.fori_loop(0, rows, norm_step, (zero, zero, zero))
    for k in range(3):
        sums_ref[k : k + 1, :] = jnp.sum(sums[k], axis=0, keepdims=True)
    sums_ref[3:8, :] = jnp.zeros((5, chans), f32)


def back_kernel(gd_ref, g_ref, wexp, gi_ref):
    rows, cols, chans = g_ref.shape
    blocks = chans // LANES
    half = cols // 4

    def conv_step(c, carry):
        lanes = pl.ds(pl.multiple_of(c * LANES, LANES), LANES)
        for part in range(4):
            acc = conv_block(gd_ref, c, wexp, rows, part * half, half, True)
            for h in range(rows):
                span = slice(part * half, part * half + half)
                gi_ref[h, span, lanes] = (g_ref[h, span, lanes].astype(f32) + acc[h].reshape(half, LANES)).astype(bf16)
        return carry

    lax.fori_loop(0, blocks, conv_step, 0)


def tap_kernel(xp_ref, gd_ref, vecs_ref, sums_ref, *rest, taps, fast):
    *more, small_ref = rest
    blocks, rows, padded, _ = xp_ref.shape
    cols = padded - 2 * EDGE
    chans = blocks * LANES

    def step(c, carry):
        lanes = pl.ds(pl.multiple_of(c * LANES, LANES), LANES)
        for j in range(7):
            acc = [None] * 7
            for b in range(0, cols, 16):
                grads = [gd_ref[c, h, EDGE + b : EDGE + b + 16, :].reshape(2, 8, LANES) for h in range(rows)]
                for hp in range(rows):
                    at = EDGE + b + j - 3
                    piece = xp_ref[c, hp, at : at + 16, :].reshape(2, 8, LANES)
                    for h in range(max(0, hp - 3), min(rows, hp + 4)):
                        i = hp - h + 3
                        term = grads[h] * piece
                        term = term[0] + term[1]
                        acc[i] = term if acc[i] is None else acc[i] + term
            for i in range(7):
                small_ref[7 * i + j : 7 * i + j + 1, lanes] = jnp.sum(acc[i], axis=0, keepdims=True)
        return carry

    small_ref[taps:, :] = jnp.zeros((small_ref.shape[0] - taps, chans), f32)
    lax.fori_loop(0, blocks, step, 0)
    small_ref[taps : taps + 3, :] = sums_ref[0:3, :]
    small_ref[taps + 3 : taps + 4, :] = vecs_ref[3:4, :]
    if fast:
        scales, bsums = more[:4], more[4:]
        total = scales[0][...] + scales[1][...] + scales[2][...] + scales[3][...]
        row = jnp.sum(total, axis=0, keepdims=True) / vecs_ref[1:2, :] + vecs_ref[2:3, :] * vecs_ref[4:5, :]
        small_ref[taps + 4 : taps + 5, :] = row
        chip, _ = place()
        for k in range(4):
            small_ref[pl.ds(taps + 5 + lax.bitwise_xor(chip, k), 1), :] = bsums[k][0:1, :]


def merge_kernel(o1_ref, o2_ref, x_ref, y_ref, gi_ref, out1_ref, out2_ref, recv_hbm, sem, *, factor):
    part = o1_ref.shape[0]
    move = pltpu.make_async_copy(gi_ref, recv_hbm, sem)
    move.start()
    out1_ref[...] = (o1_ref[...] + x_ref[0:part, :].astype(f32) + y_ref[part:, :].astype(f32)) * factor
    out2_ref[...] = ((o2_ref[...] + x_ref[part:, :].astype(f32) + y_ref[0:part, :].astype(f32)) * factor).T
    move.wait()


def pair_kernel(own_ref, got_ref, total_ref, sent_ref):
    total = own_ref[...] + got_ref[...]
    total_ref[...] = total
    sent_ref[...] = total.astype(bf16)


def small_kernel(total_ref, a_ref, b_ref, c_ref, bias_ref, small_ref, stage_ref, *, factor):
    chans = total_ref.shape[1]
    rows = small_ref.shape[0]
    more = a_ref[...].astype(f32) + b_ref[...].astype(f32) + c_ref[...].astype(f32)
    stage_ref[...] = (total_ref[...] + more) * factor
    for k in range(rows):
        small_ref[k] = stage_ref[k : k + 1, :]
    for k in range(bias_ref.shape[1] // chans):
        bias_ref[:, k * chans : (k + 1) * chans] = stage_ref[rows + k : rows + k + 1, :]


def shifted(block, axis, distance):
    devices = range(lax.axis_size(axis))
    route = [(i - distance, i) for i in devices if i - distance in devices]
    return lax.ppermute(block, axis, route)


def swap(value, bit, count):
    return lax.ppermute(value, "dp", [(i, i ^ bit) for i in range(count)])


def shards(
    block_input,
    grad_output,
    depth_weight,
    depth_bias,
    norm_gain,
    norm_shift,
    pw1_weight,
    pw1_bias,
    pw2_weight,
    pw2_bias,
    layer_scale,
):
    x, g = block_input[0, 0], grad_output[0, 0]
    rows, cols, chans = x.shape
    cells = rows * cols
    blocks = chans // LANES
    taps = depth_weight.shape[1]
    w1, w2 = pw1_weight[0], pw2_weight[0]
    units = w1.shape[0]
    replicas = lax.axis_size("dp")
    factor = 1.0 / replicas
    wide = 768
    part = wide // 2
    fast = replicas == 8 and units == 4 * wide

    wexp = struct((blocks, taps + 42, 8, LANES), f32)
    padded = struct((blocks, rows, cols + 2 * EDGE, LANES), f32)
    like = lambda v: struct(v.shape, v.dtype)
    hbm = pl.BlockSpec(memory_space=pltpu.HBM)
    pin = lambda *vs: tuple(pltpu.with_memory_space_constraint(v, pltpu.HBM) for v in vs)
    vmem = pl.BlockSpec(memory_space=pltpu.VMEM)
    gp, xp, vecs, wexp, gv, tmp = call(
        load_kernel,
        (struct((cells, chans), bf16), padded, struct((8, chans), f32), wexp, like(g), struct((8, chans), f32)),
        *pin(x, g, depth_weight[0], depth_bias, norm_gain, norm_shift, layer_scale, pw2_bias),
        name="load", in_specs=[hbm] * 8, cost=estimate(1e10, 1e6),
        scratch=[pltpu.VMEM(x.shape, bf16), pltpu.VMEM((taps, chans), bf16), pltpu.SemaphoreType.DMA((8,))],
    )
    yn, normed, rstd, w1, b1, w2 = call(
        front_kernel,
        (struct((cells, chans), bf16), struct((cells, chans), f32), struct((cells, LANES), f32),
         like(w1), like(pw1_bias), like(w2)),
        xp, wexp, tmp, *pin(w1, pw1_bias, w2),
        name="front", in_specs=[vmem] * 3 + [hbm] * 3, cost=estimate(1e10, 1e6),
        scratch=[pltpu.VMEM((cells, LANES), f32), pltpu.SemaphoreType.DMA((3,))],
    )

    def wide_step(slot, mode, *more, other=None):
        sums = struct((8, wide), f32)
        outs = (struct((cells, chans), f32),) + ((sums,) if mode == "join" else ()) + (
            sums, struct((wide, cells), bf16), struct((wide, cells), bf16))
        return call(
            lambda *refs: wide_kernel(*refs, mode=mode, slot=slot, other=other), outs, yn, gp, w1, b1, w2, *more,
            name="wide", aliases={5: 0} if mode == "next" else {}, cost=estimate(1e10, 1e6),
        )

    def flip(k):
        return lambda chip: lax.bitwise_xor(chip, k)

    def slope(gn):
        return call(slope_kernel, (padded, struct((8, chans), f32)), gn, normed, rstd, vecs,
                    name="slope", cost=estimate(1e6, 1e3))

    if fast:
        gp_s, yn_s = swap(gp, 1, replicas), swap(yn, 1, replicas)
        part_rows = struct((part, cells), bf16)

        def share(k, keep, got, types):
            outs = (struct((part, chans), types[0]), struct((part, chans), types[1]), struct((8, chans), f32))
            return call(lambda *refs: share_kernel(*refs, slot=flip(k)), outs,
                        w2, yn, yn_s, gp, gp_s, keep, got, name="share", cost=estimate(1e6, 1e3))

        rise, keep_h, send_h = call(
            lambda *refs: open_kernel(*refs, slot=flip(3)), (struct((cells, wide), f32), part_rows, part_rows),
            yn, w1, b1, name="open", cost=estimate(1e6, 1e3))
        got_h = swap(send_h, 1, replicas)
        gpre, keep_g, send_g = call(
            lambda *refs: close_kernel(*refs, slot=flip(3)), (struct((cells, wide), bf16), part_rows, part_rows),
            gp, rise, w2, name="close", cost=estimate(1e6, 1e3))
        got_g = swap(send_g, 1, replicas)
        grad = struct((part, chans), bf16)
        gpre, got_h = lax.optimization_barrier((gpre, got_h))
        d2, sc_d = call(lambda *refs: half_kernel(*refs, slot=flip(3)), (grad, struct((8, chans), f32)),
                        gp, gp_s, keep_h, got_h, w2, name="half", cost=estimate(1e6, 1e3))
        d2, got_g = lax.optimization_barrier((d2, got_g))
        d1 = call(lambda *refs: half_kernel(*refs, slot=None), (grad,), yn, yn_s, keep_g, got_g,
                  name="half", cost=estimate(1e6, 1e3))[0]
        gpre, d1 = lax.optimization_barrier((gpre, d1))
        d1_in, d2_in = swap(d1, 2, replicas), swap(d2, 4, replicas)
        gn, bd, bx, keep_x, send_x = wide_step(flip(1), "join", gpre, other=flip(3))
        got_x = swap(send_x, 1, replicas)
        gn, by, keep_y, send_y = wide_step(flip(2), "next", gn)
        got_y = swap(send_y, 1, replicas)
        gn, bo, keep_o, send_o = wide_step(flip(0), "next", gn)
        got_o = swap(send_o, 1, replicas)
        gn, got_x = lax.optimization_barrier((gn, got_x))
        x1, x2, sc_x = share(1, keep_x, got_x, (bf16, f32))
        x1, got_y = lax.optimization_barrier((x1, got_y))
        y1, y2, sc_y = share(2, keep_y, got_y, (f32, bf16))
        y1, gn = lax.optimization_barrier((y1, gn))
        gd, sums = slope(gn)
        gd, x1, x2, y1, y2, d1_in, d2_in = lax.optimization_barrier((gd, x1, x2, y1, y2, d1_in, d2_in))

        def relay(direct, base, more):
            return call(relay_kernel, struct((wide, chans), bf16), direct, base, more,
                        name="relay", cost=estimate(1e6, 1e3))

        pack_x = relay(x1, x2, d2_in)
        y2, pack_x = lax.optimization_barrier((y2, pack_x))
        pack_y = relay(y2, y1, d1_in)
        gd, pack_y = lax.optimization_barrier((gd, pack_y))
        x_in, y_in = swap(pack_x, 2, replicas), swap(pack_y, 4, replicas)
    else:
        core = lax.axis_index("dp") % 2
        gn, bsums, g1, g2 = None, [], [], []
        for p in range(units // wide):
            gn, bsum, keep, send = wide_step(lambda chip, p=p: jnp.int32(p), *(("next", gn) if p else ("first",)))
            lo, hi = jnp.where(core == 0, keep, send), jnp.where(core == 0, send, keep)
            bsums.append(bsum[0:1])
            g1 += [dot(v[:part], yn) for v in (lo, hi)]
            g2 += [dot(v[part:], gp) for v in (lo, hi)]
        g1, g2 = jnp.concatenate(g1, axis=0), jnp.concatenate(g2, axis=0).T

    if not fast:
        gd, sums = slope(gn)
    gi = call(back_kernel, struct((rows, cols, chans), bf16), gd, gv, wexp, name="back", cost=estimate(1e6, 1e3))
    received = shifted(gi, "section", -1)

    if fast:
        o1, o2, sc_o = share(0, keep_o, got_o, (f32, f32))
        more = (sc_d, sc_x, sc_y, sc_o, bo, bx, by, bd)
    else:
        more = ()
    total_rows = -(-(taps + 5 + units // chans) // 8) * 8
    small = call(lambda *refs: tap_kernel(*refs, taps=taps, fast=fast), struct((total_rows, chans), f32),
                 xp, gd, vecs, sums, *more, name="taps", cost=estimate(1e6, 1e3))

    if fast:
        rows_all = struct(small.shape, f32)
        total, sent = call(pair_kernel, (rows_all, struct(small.shape, bf16)), small, swap(small, 1, replicas),
                           name="pair", cost=estimate(1e6, 1e3))
        parts = [swap(sent, bits, replicas) for bits in (2, 4)]
        sent, received = lax.optimization_barrier((sent, received))
        parts.append(swap(sent, 6, replicas))
        out1, out2, received = pl.pallas_call(
            lambda *refs: merge_kernel(*refs, factor=factor),
            out_shape=(struct((part, chans), f32), struct((chans, part), f32), like(gi)),
            in_specs=[vmem] * 5,
            out_specs=(vmem, vmem, hbm),
            scratch_shapes=[pltpu.SemaphoreType.DMA],
            compiler_params=pltpu.CompilerParams(vmem_limit_bytes=VMEM_LIMIT),
            name="merge",
        )(o1, o2, x_in, y_in, received)
        out1, total = lax.optimization_barrier((out1, total))
        bias, small = call(
            lambda *refs: small_kernel(*refs, factor=factor),
            (struct((1, units), f32), struct((taps + 5, 1, chans), f32)), total, *parts,
            name="small", scratch=[pltpu.VMEM(small.shape, f32)], cost=estimate(1e6, 1e3))
        small = jnp.transpose(small, (1, 0, 2))
    else:
        scale_sum = jnp.sum(g2 * w2.astype(f32), axis=1)
        gscale = scale_sum / layer_scale[0] + pw2_bias[0] * vecs[4]
        small = jnp.concatenate([small[: taps + 4], gscale[None], *bsums], axis=0)
        small = lax.psum(small, "dp")
        out1 = lax.psum_scatter(g1, "dp", scatter_dimension=0, tiled=True) * factor
        out2 = lax.psum_scatter(g2, "dp", scatter_dimension=1, tiled=True) * factor
        small = small * factor
        bias, small = small[taps + 5 :].reshape(1, -1), small[None, : taps + 5]
    return (out1[None], out2[None], bias, small, received[None, None])


def solution(mesh):
    in_specs = (
        P("section", "dp", None, None, None),
        P("section", "dp", None, None, None),
        P("section", None, None),
        P("section", None),
        P("section", None),
        P("section", None),
        P("section", None, None),
        P("section", None),
        P("section", None, None),
        P("section", None),
        P("section", None),
    )
    out_specs = (
        P("section", "dp", None),
        P("section", None, "dp"),
        P("section", None),
        P("section", None, None),
        P("section", "dp", None, None, None),
    )
    return jax.shard_map(shards, mesh=mesh, in_specs=in_specs, out_specs=out_specs, check_vma=False)
```

```python
import jax
import jax.numpy as jnp
from jax import lax
from jax.experimental import pallas as pl
from jax.experimental.pallas import tpu as pltpu
from jax.sharding import PartitionSpec as P

root_half = 0.7071067811865476
inv_root_two_pi = 0.3989422804014327
f32 = jnp.float32
bf16 = jnp.bfloat16
LANES = 128
EDGE = 8
VMEM_LIMIT = 12 * 1024 * 1024


def struct(shape, dtype):
    return jax.ShapeDtypeStruct(shape, dtype)


def call(body, out_shape, *args, name, aliases=None, scratch=(), scalars=0, in_specs=None, cost=None):
    vmem = pl.BlockSpec(memory_space=pltpu.VMEM)
    smem = pl.BlockSpec(memory_space=pltpu.SMEM)
    specs = [smem] * scalars + [vmem] * (len(args) - scalars) if in_specs is None else in_specs
    return pl.pallas_call(
        body,
        out_shape=out_shape,
        in_specs=specs,
        out_specs=jax.tree.map(lambda _: vmem, out_shape),
        scratch_shapes=list(scratch),
        input_output_aliases=aliases or {},
        compiler_params=pltpu.CompilerParams(vmem_limit_bytes=VMEM_LIMIT),
        cost_estimate=cost,
        name=name,
    )(*args)


def estimate(flops, nbytes):
    return pl.CostEstimate(flops=int(flops), transcendentals=0, bytes_accessed=int(nbytes))


def dot(a, b):
    return jnp.dot(a, b, preferred_element_type=f32)


def dot_last(a, b):
    return lax.dot_general(a, b, (((1,), (1,)), ((), ())), preferred_element_type=f32)


def place():
    me = lax.axis_index("dp")
    return lax.shift_right_logical(me, 1), lax.bitwise_and(me, 1)


def expand_taps(w_ref, wexp, blocks):
    count = w_ref.shape[0]
    for c in range(blocks):
        rows = [w_ref[k : k + 1, c * LANES : (c + 1) * LANES].astype(f32) for k in range(count)]
        for k in range(count):
            wexp[c, k] = jnp.broadcast_to(rows[k], (8, LANES))
        for i in range(6):
            for j in range(7):
                wexp[c, count + 7 * i + j] = jnp.broadcast_to(rows[7 * i + j] + rows[7 * i + 7 + j], (8, LANES))


def zero_edges(buf, blocks, rows, cols):
    zero = jnp.zeros((rows, EDGE, LANES), f32)
    for c in range(blocks):
        buf[c, :, 0:EDGE, :] = zero
        buf[c, :, EDGE + cols : EDGE + cols + EDGE, :] = zero


def conv_block(src, c, wexp, rows, start, width, flip):
    groups = width // 8
    pairs = rows // 2
    tap = lambda k: 3 - k if flip else k + 3
    lone = lambda k, j: wexp[c, 7 * tap(k) + j]
    both = lambda k, j: wexp[c, 49 + 7 * min(tap(k), tap(k + 1)) + j]
    odd, even, mixed = [None] * pairs, [None] * (pairs + 1), [None] * pairs

    def put(acc, a, term):
        acc[a] = term if acc[a] is None else acc[a] + term

    for j in range(7):
        at = start + EDGE + (3 - j if flip else j - 3)
        for b in range(pairs):
            x0, x1 = (src[c, 2 * b + k, at : at + width, :].reshape(groups, 8, LANES) for k in range(2))
            for d in range(-1, 2):
                if 0 <= b - d < pairs:
                    put(odd, b - d, x1 * lone(2 * d, j))
            for d in range(-2, 2):
                if 0 <= b - d <= pairs:
                    put(even, b - d, x0 * lone(2 * d + 1, j))
            x0 = x0 + x1
            for d in range(-2, 2):
                if 0 <= b - d < pairs:
                    put(mixed, b - d, x0 * (lone(-3, j) if d == -2 else both(2 * d, j)))
    acc = []
    for a in range(pairs):
        acc += [mixed[a] - odd[a] - even[a], odd[a] + even[a + 1]]
    return acc


def load_kernel(x_hbm, g_hbm, w_hbm, db_hbm, gain_hbm, shift_hbm, scale_hbm, bb_hbm,
                gp_ref, xp_ref, vecs_ref, wexp, g_ref, tmp_ref, x_ref, w_ref, sems):
    rows, cols, chans = x_ref.shape
    blocks = chans // LANES
    moves = [(w_hbm, w_ref), (scale_hbm, tmp_ref.at[3:4]), (g_hbm, g_ref), (x_hbm, x_ref), (db_hbm, tmp_ref.at[0:1]),
             (gain_hbm, tmp_ref.at[1:2]), (shift_hbm, tmp_ref.at[2:3]), (bb_hbm, tmp_ref.at[4:5])]
    copies = [pltpu.make_async_copy(src, dst, sems.at[k]) for k, (src, dst) in enumerate(moves)]
    for copy in copies:
        copy.start()
    zero_edges(xp_ref, blocks, rows, cols)
    copies[0].wait()
    expand_taps(w_ref, wexp, blocks)
    copies[1].wait()
    copies[2].wait()
    b2, gs = [], []
    for c in range(blocks):
        lanes = slice(c * LANES, (c + 1) * LANES)
        g = g_ref[:, :, lanes].astype(f32).reshape(rows * cols, LANES)
        gp = (g * tmp_ref[3:4, lanes]).astype(bf16)
        gp_ref[:, lanes] = gp
        b2.append(jnp.sum(gp.astype(f32), axis=0, keepdims=True))
        gs.append(jnp.sum(g, axis=0, keepdims=True))
    copies[3].wait()
    for c in range(blocks):
        xp_ref[c, :, EDGE : EDGE + cols, :] = x_ref[:, :, c * LANES : (c + 1) * LANES].astype(f32)
    for copy in copies[4:]:
        copy.wait()
    vecs_ref[0:1, :] = tmp_ref[1:2, :]
    vecs_ref[1:2, :] = tmp_ref[3:4, :]
    vecs_ref[2:3, :] = tmp_ref[4:5, :]
    vecs_ref[3:4, :] = jnp.concatenate(b2, axis=1)
    vecs_ref[4:5, :] = jnp.concatenate(gs, axis=1)
    vecs_ref[5:8, :] = jnp.zeros((3, chans), f32)


def front_kernel(xp_ref, wexp, tmp_ref, w1_hbm, b1_hbm, w2_hbm,
                 yn_ref, normed_ref, rstd_ref, w1_ref, b1_ref, w2_ref, mean_ref, sems):
    blocks, rows, padded, _ = xp_ref.shape
    cols = padded - 2 * EDGE
    chans = blocks * LANES
    half = cols // 4
    moves = [(w1_hbm, w1_ref), (b1_hbm, b1_ref), (w2_hbm, w2_ref)]
    copies = [pltpu.make_async_copy(src, dst, sems.at[k]) for k, (src, dst) in enumerate(moves)]
    for copy in copies:
        copy.start()
    mean_ref[...] = jnp.zeros(mean_ref.shape, f32)

    def conv_step(c, carry):
        lanes = pl.ds(pl.multiple_of(c * LANES, LANES), LANES)
        for part in range(4):
            acc = conv_block(xp_ref, c, wexp, rows, part * half, half, False)
            bias = tmp_ref[0:1, lanes]
            for h in range(rows):
                at = slice(h * cols + part * half, h * cols + part * half + half)
                value = acc[h].reshape(half, LANES) + bias
                normed_ref[at, lanes] = value
                mean_ref[at, :] = mean_ref[at, :] + value
        return carry

    lax.fori_loop(0, blocks, conv_step, 0)
    mean_ref[...] = jnp.broadcast_to(jnp.sum(mean_ref[...], axis=-1, keepdims=True) * (1.0 / chans), mean_ref.shape)

    def spread_step(r, carry):
        at = pl.ds(pl.multiple_of(r * cols, cols), cols)
        mean = mean_ref[at, :]
        total = jnp.zeros((cols, LANES), f32)
        for c in range(blocks):
            d = normed_ref[at, c * LANES : (c + 1) * LANES] - mean
            total = total + d * d
        rstd_ref[at, :] = total
        return carry

    lax.fori_loop(0, rows, spread_step, 0)
    var = jnp.sum(rstd_ref[...], axis=-1, keepdims=True) * (1.0 / chans)
    rstd_ref[...] = jnp.broadcast_to(lax.rsqrt(var + 1e-06), rstd_ref.shape)
    gain, shift = tmp_ref[1:2, :], tmp_ref[2:3, :]

    def norm_step(r, carry):
        at = pl.ds(pl.multiple_of(r * cols, cols), cols)
        mean, rs = mean_ref[at, :], rstd_ref[at, :]
        for c in range(blocks):
            lanes = slice(c * LANES, (c + 1) * LANES)
            normed = (normed_ref[at, lanes] - mean) * rs
            normed_ref[at, lanes] = normed
            yn_ref[at, lanes] = (normed * gain[:, lanes] + shift[:, lanes]).astype(bf16)
        return carry

    lax.fori_loop(0, rows, norm_step, 0)
    for copy in copies:
        copy.wait()


def gate(pre):
    return 0.5 * (1.0 + lax.erf(pre * root_half))


def split_store(core, part, value, keep_ref, send_ref, row):
    for side in range(2):
        @pl.when(core == side)
        def _(side=side):
            k, s = side * part, (1 - side) * part
            keep_ref[row : row + part, :] = value[k : k + part, :]
            send_ref[row : row + part, :] = value[s : s + part, :]


def slope_of(pre, cdf):
    density = jnp.exp(-0.5 * pre * pre) * inv_root_two_pi
    return cdf + pre * density


def open_kernel(yn_ref, w1_ref, b1_ref, rise_ref, keep_ref, send_ref, *, slot):
    wide = rise_ref.shape[1]
    chip, core = place()
    at = pl.multiple_of(slot(chip) * wide, wide)
    pre = dot_last(yn_ref[...], w1_ref[pl.ds(at, wide), :]) + b1_ref[:, pl.ds(at, wide)]
    cdf = gate(pre)
    rise_ref[...] = slope_of(pre, cdf)
    split_store(core, wide // 2, (pre * cdf).astype(bf16).T, keep_ref, send_ref, 0)


def close_kernel(gp_ref, rise_ref, w2_ref, gpre_ref, keep_ref, send_ref, *, slot):
    wide = rise_ref.shape[1]
    chip, core = place()
    at = pl.multiple_of(slot(chip) * wide, wide)
    gpre = (dot(gp_ref[...], w2_ref[:, pl.ds(at, wide)]) * rise_ref[...]).astype(bf16)
    gpre_ref[...] = gpre
    split_store(core, wide // 2, gpre.T, keep_ref, send_ref, 0)


def wide_kernel(yn_ref, gp_ref, w1_ref, b1_ref, w2_ref, *rest, mode, slot, other):
    *more, bsum_ref, keep_ref, send_ref = rest
    wide = bsum_ref.shape[1]
    part = wide // 2
    chip, core = place()
    at = pl.multiple_of(slot(chip) * wide, wide)
    w1 = w1_ref[pl.ds(at, wide), :]
    w2 = w2_ref[:, pl.ds(at, wide)]
    pre = dot_last(yn_ref[...], w1) + b1_ref[:, pl.ds(at, wide)]
    cdf = gate(pre)
    hidden = (pre * cdf).astype(bf16)
    gpre = (dot(gp_ref[...], w2) * slope_of(pre, cdf)).astype(bf16)
    bsum_ref[...] = jnp.broadcast_to(jnp.sum(gpre.astype(f32), axis=0, keepdims=True), (8, wide))
    gn = dot(gpre, w1)
    if mode == "first":
        (gn_ref,) = more
        gn_ref[...] = gn
    elif mode == "next":
        gin_ref, gn_ref = more
        gn_ref[...] = gin_ref[...] + gn
    else:
        gpre_ref, gn_ref, osum_ref = more
        back = pl.multiple_of(other(chip) * wide, wide)
        gn_ref[...] = gn + dot(gpre_ref[...], w1_ref[pl.ds(back, wide), :])
        total = jnp.sum(gpre_ref[...].astype(f32), axis=0, keepdims=True)
        osum_ref[...] = jnp.broadcast_to(total, (8, wide))
    split_store(core, part, gpre.T, keep_ref, send_ref, 0)
    split_store(core, part, hidden.T, keep_ref, send_ref, part)


def half_kernel(own_ref, sib_ref, keep_ref, got_ref, *rest, slot):
    if slot is None:
        (d_ref,) = rest
    else:
        w2_ref, d_ref, scale_ref = rest
    d = dot(keep_ref[...], own_ref[...]) + dot(got_ref[...], sib_ref[...])
    d_ref[...] = d.astype(d_ref.dtype)
    if slot is not None:
        part, chans = d.shape
        chip, core = place()
        at = pl.multiple_of((2 * slot(chip) + core) * part, part)
        prod = d * w2_ref[:, pl.ds(at, part)].T.astype(f32)
        scale_ref[...] = jnp.sum(prod.reshape(part // 8, 8, chans), axis=0)


def share_kernel(w2_ref, yo_ref, ys_ref, go_ref, gs_ref, keep_ref, got_ref, d1_ref, d2_ref, scale_ref, *, slot):
    part = keep_ref.shape[0] // 2
    first, second = slice(0, part), slice(part, 2 * part)
    half_kernel(yo_ref, ys_ref, keep_ref.at[first, :], got_ref.at[first, :], d1_ref, slot=None)
    half_kernel(go_ref, gs_ref, keep_ref.at[second, :], got_ref.at[second, :], w2_ref, d2_ref, scale_ref, slot=slot)


def relay_kernel(direct_ref, base_ref, more_ref, pack_ref):
    part = direct_ref.shape[0]
    pack_ref[0:part, :] = direct_ref[...]
    pack_ref[part:, :] = (base_ref[...] + more_ref[...].astype(f32)).astype(bf16)


def slope_kernel(gn_ref, normed_ref, rstd_ref, vecs_ref, gd_ref, sums_ref):
    blocks, rows, padded, _ = gd_ref.shape
    cols = padded - 2 * EDGE
    chans = blocks * LANES
    zero_edges(gd_ref, blocks, rows, cols)
    gain = vecs_ref[0:1, :]

    def norm_step(r, carry):
        at = pl.ds(pl.multiple_of(r * cols, cols), cols)
        gn = gn_ref[at, :]
        normed = normed_ref[at, :]
        prod = gn * normed
        scaled = gn * gain
        mean_a = jnp.mean(scaled, axis=-1, keepdims=True)
        mean_b = jnp.mean(prod * gain, axis=-1, keepdims=True)
        rs = rstd_ref[at, 0:1]
        gd = rs * (scaled - mean_a - normed * mean_b)
        for c in range(blocks):
            gd_ref[c, r, EDGE : EDGE + cols, :] = gd[:, c * LANES : (c + 1) * LANES]
        fold = lambda v: jnp.sum(v.reshape(cols // 8, 8, chans), axis=0)
        return carry[0] + fold(gd), carry[1] + fold(prod), carry[2] + fold(gn)

    zero = jnp.zeros((8, chans), f32)
    sums = lax.fori_loop(0, rows, norm_step, (zero, zero, zero))
    for k in range(3):
        sums_ref[k : k + 1, :] = jnp.sum(sums[k], axis=0, keepdims=True)
    sums_ref[3:8, :] = jnp.zeros((5, chans), f32)


def back_kernel(gd_ref, g_ref, wexp, gi_ref):
    rows, cols, chans = g_ref.shape
    blocks = chans // LANES
    half = cols // 4

    def conv_step(c, carry):
        lanes = pl.ds(pl.multiple_of(c * LANES, LANES), LANES)
        for part in range(4):
            acc = conv_block(gd_ref, c, wexp, rows, part * half, half, True)
            for h in range(rows):
                span = slice(part * half, part * half + half)
                gi_ref[h, span, lanes] = (g_ref[h, span, lanes].astype(f32) + acc[h].reshape(half, LANES)).astype(bf16)
        return carry

    lax.fori_loop(0, blocks, conv_step, 0)


def tap_kernel(xp_ref, gd_ref, vecs_ref, sums_ref, *rest, taps, fast):
    *more, small_ref = rest
    blocks, rows, padded, _ = xp_ref.shape
    cols = padded - 2 * EDGE
    chans = blocks * LANES

    def step(c, carry):
        lanes = pl.ds(pl.multiple_of(c * LANES, LANES), LANES)
        for j in range(7):
            acc = [None] * 7
            for b in range(0, cols, 16):
                grads = [gd_ref[c, h, EDGE + b : EDGE + b + 16, :].reshape(2, 8, LANES) for h in range(rows)]
                for hp in range(rows):
                    at = EDGE + b + j - 3
                    piece = xp_ref[c, hp, at : at + 16, :].reshape(2, 8, LANES)
                    for h in range(max(0, hp - 3), min(rows, hp + 4)):
                        i = hp - h + 3
                        term = grads[h] * piece
                        term = term[0] + term[1]
                        acc[i] = term if acc[i] is None else acc[i] + term
            for i in range(7):
                small_ref[7 * i + j : 7 * i + j + 1, lanes] = jnp.sum(acc[i], axis=0, keepdims=True)
        return carry

    small_ref[taps:, :] = jnp.zeros((small_ref.shape[0] - taps, chans), f32)
    lax.fori_loop(0, blocks, step, 0)
    small_ref[taps : taps + 3, :] = sums_ref[0:3, :]
    small_ref[taps + 3 : taps + 4, :] = vecs_ref[3:4, :]
    if fast:
        scales, bsums = more[:4], more[4:]
        total = scales[0][...] + scales[1][...] + scales[2][...] + scales[3][...]
        row = jnp.sum(total, axis=0, keepdims=True) / vecs_ref[1:2, :] + vecs_ref[2:3, :] * vecs_ref[4:5, :]
        small_ref[taps + 4 : taps + 5, :] = row
        chip, _ = place()
        for k in range(4):
            small_ref[pl.ds(taps + 5 + lax.bitwise_xor(chip, k), 1), :] = bsums[k][0:1, :]


def merge_kernel(o1_ref, o2_ref, x_ref, y_ref, out1_ref, out2_ref, *, factor):
    part = o1_ref.shape[0]
    out1_ref[...] = (o1_ref[...] + x_ref[0:part, :].astype(f32) + y_ref[part:, :].astype(f32)) * factor
    out2_ref[...] = ((o2_ref[...] + x_ref[part:, :].astype(f32) + y_ref[0:part, :].astype(f32)) * factor).T


def pair_kernel(own_ref, got_ref, total_ref, sent_ref):
    total = own_ref[...] + got_ref[...]
    total_ref[...] = total
    sent_ref[...] = total.astype(bf16)


def gather_kernel(total_ref, near_ref, far_ref, some_ref):
    _, core = place()
    some_ref[...] = near_ref[...].astype(f32)

    @pl.when(core == 0)
    def _():
        some_ref[...] = some_ref[...] + total_ref[...] + far_ref[...].astype(f32)


def emit_kernel(gi_ref, recv_hbm, sem):
    move = pltpu.make_async_copy(gi_ref, recv_hbm, sem)
    move.start()
    move.wait()


def small_kernel(own_ref, got_ref, bias_ref, small_ref, stage_ref, *, factor):
    chans = own_ref.shape[1]
    rows = small_ref.shape[0]
    stage_ref[...] = (own_ref[...] + got_ref[...]) * factor
    for k in range(rows):
        small_ref[k] = stage_ref[k : k + 1, :]
    for k in range(bias_ref.shape[1] // chans):
        bias_ref[:, k * chans : (k + 1) * chans] = stage_ref[rows + k : rows + k + 1, :]


def shifted(block, axis, distance):
    devices = range(lax.axis_size(axis))
    route = [(i - distance, i) for i in devices if i - distance in devices]
    return lax.ppermute(block, axis, route)


def swap(value, bit, count):
    return lax.ppermute(value, "dp", [(i, i ^ bit) for i in range(count)])


def shards(
    block_input,
    grad_output,
    depth_weight,
    depth_bias,
    norm_gain,
    norm_shift,
    pw1_weight,
    pw1_bias,
    pw2_weight,
    pw2_bias,
    layer_scale,
):
    x, g = block_input[0, 0], grad_output[0, 0]
    rows, cols, chans = x.shape
    cells = rows * cols
    blocks = chans // LANES
    taps = depth_weight.shape[1]
    w1, w2 = pw1_weight[0], pw2_weight[0]
    units = w1.shape[0]
    replicas = lax.axis_size("dp")
    factor = 1.0 / replicas
    wide = 768
    part = wide // 2
    fast = replicas == 8 and units == 4 * wide

    wexp = struct((blocks, taps + 42, 8, LANES), f32)
    padded = struct((blocks, rows, cols + 2 * EDGE, LANES), f32)
    like = lambda v: struct(v.shape, v.dtype)
    hbm = pl.BlockSpec(memory_space=pltpu.HBM)
    pin = lambda *vs: tuple(pltpu.with_memory_space_constraint(v, pltpu.HBM) for v in vs)
    vmem = pl.BlockSpec(memory_space=pltpu.VMEM)
    gp, xp, vecs, wexp, gv, tmp = call(
        load_kernel,
        (struct((cells, chans), bf16), padded, struct((8, chans), f32), wexp, like(g), struct((8, chans), f32)),
        *pin(x, g, depth_weight[0], depth_bias, norm_gain, norm_shift, layer_scale, pw2_bias),
        name="load", in_specs=[hbm] * 8, cost=estimate(1e10, 1e6),
        scratch=[pltpu.VMEM(x.shape, bf16), pltpu.VMEM((taps, chans), bf16), pltpu.SemaphoreType.DMA((8,))],
    )
    yn, normed, rstd, w1, b1, w2 = call(
        front_kernel,
        (struct((cells, chans), bf16), struct((cells, chans), f32), struct((cells, LANES), f32),
         like(w1), like(pw1_bias), like(w2)),
        xp, wexp, tmp, *pin(w1, pw1_bias, w2),
        name="front", in_specs=[vmem] * 3 + [hbm] * 3, cost=estimate(1e10, 1e6),
        scratch=[pltpu.VMEM((cells, LANES), f32), pltpu.SemaphoreType.DMA((3,))],
    )

    def wide_step(slot, mode, *more, other=None):
        sums = struct((8, wide), f32)
        outs = (struct((cells, chans), f32),) + ((sums,) if mode == "join" else ()) + (
            sums, struct((wide, cells), bf16), struct((wide, cells), bf16))
        return call(
            lambda *refs: wide_kernel(*refs, mode=mode, slot=slot, other=other), outs, yn, gp, w1, b1, w2, *more,
            name="wide", aliases={5: 0} if mode == "next" else {}, cost=estimate(1e10, 1e6),
        )

    def flip(k):
        return lambda chip: lax.bitwise_xor(chip, k)

    def slope(gn):
        return call(slope_kernel, (padded, struct((8, chans), f32)), gn, normed, rstd, vecs,
                    name="slope", cost=estimate(1e6, 1e3))

    if fast:
        gp_s, yn_s = swap(gp, 1, replicas), swap(yn, 1, replicas)
        part_rows = struct((part, cells), bf16)

        def share(k, keep, got, types):
            outs = (struct((part, chans), types[0]), struct((part, chans), types[1]), struct((8, chans), f32))
            return call(lambda *refs: share_kernel(*refs, slot=flip(k)), outs,
                        w2, yn, yn_s, gp, gp_s, keep, got, name="share", cost=estimate(1e6, 1e3))

        rise, keep_h, send_h = call(
            lambda *refs: open_kernel(*refs, slot=flip(3)), (struct((cells, wide), f32), part_rows, part_rows),
            yn, w1, b1, name="open", cost=estimate(1e6, 1e3))
        got_h = swap(send_h, 1, replicas)
        gpre, keep_g, send_g = call(
            lambda *refs: close_kernel(*refs, slot=flip(3)), (struct((cells, wide), bf16), part_rows, part_rows),
            gp, rise, w2, name="close", cost=estimate(1e6, 1e3))
        got_g = swap(send_g, 1, replicas)
        grad = struct((part, chans), bf16)
        gpre, got_h = lax.optimization_barrier((gpre, got_h))
        d2, sc_d = call(lambda *refs: half_kernel(*refs, slot=flip(3)), (grad, struct((8, chans), f32)),
                        gp, gp_s, keep_h, got_h, w2, name="half", cost=estimate(1e6, 1e3))
        d2, got_g = lax.optimization_barrier((d2, got_g))
        d1 = call(lambda *refs: half_kernel(*refs, slot=None), (grad,), yn, yn_s, keep_g, got_g,
                  name="half", cost=estimate(1e6, 1e3))[0]
        gpre, d1 = lax.optimization_barrier((gpre, d1))
        d1_in, d2_in = swap(d1, 2, replicas), swap(d2, 4, replicas)
        gn, bd, bx, keep_x, send_x = wide_step(flip(1), "join", gpre, other=flip(3))
        got_x = swap(send_x, 1, replicas)
        gn, by, keep_y, send_y = wide_step(flip(2), "next", gn)
        got_y = swap(send_y, 1, replicas)
        gn, bo, keep_o, send_o = wide_step(flip(0), "next", gn)
        got_o = swap(send_o, 1, replicas)
        gn, got_x = lax.optimization_barrier((gn, got_x))
        x1, x2, sc_x = share(1, keep_x, got_x, (bf16, f32))
        x1, got_y = lax.optimization_barrier((x1, got_y))
        y1, y2, sc_y = share(2, keep_y, got_y, (f32, bf16))
        y1, gn = lax.optimization_barrier((y1, gn))
        gd, sums = slope(gn)
        gd, x1, x2, y1, y2, d1_in, d2_in = lax.optimization_barrier((gd, x1, x2, y1, y2, d1_in, d2_in))

        def relay(direct, base, more):
            return call(relay_kernel, struct((wide, chans), bf16), direct, base, more,
                        name="relay", cost=estimate(1e6, 1e3))

        pack_x = relay(x1, x2, d2_in)
        y2, pack_x = lax.optimization_barrier((y2, pack_x))
        pack_y = relay(y2, y1, d1_in)
        gd, pack_y = lax.optimization_barrier((gd, pack_y))
        x_in, y_in = swap(pack_x, 2, replicas), swap(pack_y, 4, replicas)
    else:
        core = lax.axis_index("dp") % 2
        gn, bsums, g1, g2 = None, [], [], []
        for p in range(units // wide):
            gn, bsum, keep, send = wide_step(lambda chip, p=p: jnp.int32(p), *(("next", gn) if p else ("first",)))
            lo, hi = jnp.where(core == 0, keep, send), jnp.where(core == 0, send, keep)
            bsums.append(bsum[0:1])
            g1 += [dot(v[:part], yn) for v in (lo, hi)]
            g2 += [dot(v[part:], gp) for v in (lo, hi)]
        g1, g2 = jnp.concatenate(g1, axis=0), jnp.concatenate(g2, axis=0).T

    if not fast:
        gd, sums = slope(gn)
    gi = call(back_kernel, struct((rows, cols, chans), bf16), gd, gv, wexp, name="back", cost=estimate(1e6, 1e3))
    received = shifted(gi, "section", -1)

    if fast:
        o1, o2, sc_o = share(0, keep_o, got_o, (f32, f32))
        more = (sc_d, sc_x, sc_y, sc_o, bo, bx, by, bd)
    else:
        more = ()
    total_rows = -(-(taps + 5 + units // chans) // 8) * 8
    small = call(lambda *refs: tap_kernel(*refs, taps=taps, fast=fast), struct((total_rows, chans), f32),
                 xp, gd, vecs, sums, *more, name="taps", cost=estimate(1e6, 1e3))

    if fast:
        rows_all = struct(small.shape, f32)
        total, sent = call(pair_kernel, (rows_all, struct(small.shape, bf16)), small, swap(small, 1, replicas),
                           name="pair", cost=estimate(1e6, 1e3))
        near = lax.ppermute(sent, "dp", [(i, i ^ (4 if i % 2 else 2)) for i in range(replicas)])
        far = lax.ppermute(sent, "dp", [(i, i ^ 6) for i in range(0, replicas, 2)])
        out1, out2 = call(
            lambda *refs: merge_kernel(*refs, factor=factor),
            (struct((part, chans), f32), struct((chans, part), f32)),
            o1, o2, x_in, y_in, name="merge", cost=estimate(1e6, 1e3))
        out1, total = lax.optimization_barrier((out1, total))
        some = call(gather_kernel, rows_all, total, near, far, name="gather", cost=estimate(1e6, 1e3))
        some_in = swap(some, 1, replicas)
        some, received = lax.optimization_barrier((some, received))
        received = pl.pallas_call(
            emit_kernel, out_shape=like(gi), in_specs=[vmem], out_specs=hbm,
            scratch_shapes=[pltpu.SemaphoreType.DMA],
            compiler_params=pltpu.CompilerParams(vmem_limit_bytes=VMEM_LIMIT), name="emit",
        )(received)
        some, received = lax.optimization_barrier((some, received))
        bias, small = call(
            lambda *refs: small_kernel(*refs, factor=factor),
            (struct((1, units), f32), struct((taps + 5, 1, chans), f32)), some, some_in,
            name="small", scratch=[pltpu.VMEM(small.shape, f32)], cost=estimate(1e6, 1e3))
        small = jnp.transpose(small, (1, 0, 2))
    else:
        scale_sum = jnp.sum(g2 * w2.astype(f32), axis=1)
        gscale = scale_sum / layer_scale[0] + pw2_bias[0] * vecs[4]
        small = jnp.concatenate([small[: taps + 4], gscale[None], *bsums], axis=0)
        small = lax.psum(small, "dp")
        out1 = lax.psum_scatter(g1, "dp", scatter_dimension=0, tiled=True) * factor
        out2 = lax.psum_scatter(g2, "dp", scatter_dimension=1, tiled=True) * factor
        small = small * factor
        bias, small = small[taps + 5 :].reshape(1, -1), small[None, : taps + 5]
    return (out1[None], out2[None], bias, small, received[None, None])


def solution(mesh):
    in_specs = (
        P("section", "dp", None, None, None),
        P("section", "dp", None, None, None),
        P("section", None, None),
        P("section", None),
        P("section", None),
        P("section", None),
        P("section", None, None),
        P("section", None),
        P("section", None, None),
        P("section", None),
        P("section", None),
    )
    out_specs = (
        P("section", "dp", None),
        P("section", None, "dp"),
        P("section", None),
        P("section", None, None),
        P("section", "dp", None, None, None),
    )
    return jax.shard_map(shards, mesh=mesh, in_specs=in_specs, out_specs=out_specs, check_vma=False)
```

```python
import jax
import jax.numpy as jnp
from jax import lax
from jax.experimental import pallas as pl
from jax.experimental.pallas import tpu as pltpu
from jax.sharding import PartitionSpec as P

root_half = 0.7071067811865476
inv_root_two_pi = 0.3989422804014327
f32 = jnp.float32
bf16 = jnp.bfloat16
LANES = 128
EDGE = 8
VMEM_LIMIT = 12 * 1024 * 1024


def struct(shape, dtype):
    return jax.ShapeDtypeStruct(shape, dtype)


def call(body, out_shape, *args, name, aliases=None, scratch=(), scalars=0, in_specs=None, cost=None):
    vmem = pl.BlockSpec(memory_space=pltpu.VMEM)
    smem = pl.BlockSpec(memory_space=pltpu.SMEM)
    specs = [smem] * scalars + [vmem] * (len(args) - scalars) if in_specs is None else in_specs
    return pl.pallas_call(
        body,
        out_shape=out_shape,
        in_specs=specs,
        out_specs=jax.tree.map(lambda _: vmem, out_shape),
        scratch_shapes=list(scratch),
        input_output_aliases=aliases or {},
        compiler_params=pltpu.CompilerParams(vmem_limit_bytes=VMEM_LIMIT),
        cost_estimate=cost,
        name=name,
    )(*args)


def estimate(flops, nbytes):
    return pl.CostEstimate(flops=int(flops), transcendentals=0, bytes_accessed=int(nbytes))


def dot(a, b):
    return jnp.dot(a, b, preferred_element_type=f32)


def dot_last(a, b):
    return lax.dot_general(a, b, (((1,), (1,)), ((), ())), preferred_element_type=f32)


def place():
    me = lax.axis_index("dp")
    return lax.shift_right_logical(me, 1), lax.bitwise_and(me, 1)


def expand_taps(w_ref, wexp, blocks):
    count = w_ref.shape[0]
    for c in range(blocks):
        rows = [w_ref[k : k + 1, c * LANES : (c + 1) * LANES].astype(f32) for k in range(count)]
        for k in range(count):
            wexp[c, k] = jnp.broadcast_to(rows[k], (8, LANES))
        for i in range(6):
            for j in range(7):
                wexp[c, count + 7 * i + j] = jnp.broadcast_to(rows[7 * i + j] + rows[7 * i + 7 + j], (8, LANES))


def zero_edges(buf, blocks, rows, cols):
    zero = jnp.zeros((rows, EDGE, LANES), f32)
    for c in range(blocks):
        buf[c, :, 0:EDGE, :] = zero
        buf[c, :, EDGE + cols : EDGE + cols + EDGE, :] = zero


def conv_block(src, c, wexp, rows, start, width, flip):
    groups = width // 8
    pairs = rows // 2
    tap = lambda k: 3 - k if flip else k + 3
    lone = lambda k, j: wexp[c, 7 * tap(k) + j]
    both = lambda k, j: wexp[c, 49 + 7 * min(tap(k), tap(k + 1)) + j]
    odd, even, mixed = [None] * pairs, [None] * (pairs + 1), [None] * pairs

    def put(acc, a, term):
        acc[a] = term if acc[a] is None else acc[a] + term

    for j in range(7):
        at = start + EDGE + (3 - j if flip else j - 3)
        for b in range(pairs):
            x0, x1 = (src[c, 2 * b + k, at : at + width, :].reshape(groups, 8, LANES) for k in range(2))
            for d in range(-1, 2):
                if 0 <= b - d < pairs:
                    put(odd, b - d, x1 * lone(2 * d, j))
            for d in range(-2, 2):
                if 0 <= b - d <= pairs:
                    put(even, b - d, x0 * lone(2 * d + 1, j))
            x0 = x0 + x1
            for d in range(-2, 2):
                if 0 <= b - d < pairs:
                    put(mixed, b - d, x0 * (lone(-3, j) if d == -2 else both(2 * d, j)))
    acc = []
    for a in range(pairs):
        acc += [mixed[a] - odd[a] - even[a], odd[a] + even[a + 1]]
    return acc


def load_kernel(x_hbm, g_hbm, w_hbm, db_hbm, gain_hbm, shift_hbm, scale_hbm, bb_hbm,
                gp_ref, xp_ref, vecs_ref, wexp, g_ref, tmp_ref, x_ref, w_ref, sems):
    rows, cols, chans = x_ref.shape
    blocks = chans // LANES
    moves = [(w_hbm, w_ref), (scale_hbm, tmp_ref.at[3:4]), (g_hbm, g_ref), (x_hbm, x_ref), (db_hbm, tmp_ref.at[0:1]),
             (gain_hbm, tmp_ref.at[1:2]), (shift_hbm, tmp_ref.at[2:3]), (bb_hbm, tmp_ref.at[4:5])]
    copies = [pltpu.make_async_copy(src, dst, sems.at[k]) for k, (src, dst) in enumerate(moves)]
    for copy in copies:
        copy.start()
    zero_edges(xp_ref, blocks, rows, cols)
    copies[0].wait()
    expand_taps(w_ref, wexp, blocks)
    copies[1].wait()
    copies[2].wait()
    for c in range(blocks):
        lanes = slice(c * LANES, (c + 1) * LANES)
        g = g_ref[:, :, lanes].astype(f32).reshape(rows * cols, LANES)
        gp_ref[:, lanes] = (g * tmp_ref[3:4, lanes]).astype(bf16)
    copies[3].wait()
    for c in range(blocks):
        xp_ref[c, :, EDGE : EDGE + cols, :] = x_ref[:, :, c * LANES : (c + 1) * LANES].astype(f32)
    for copy in copies[4:]:
        copy.wait()
    vecs_ref[0:1, :] = tmp_ref[1:2, :]
    vecs_ref[1:2, :] = tmp_ref[3:4, :]
    vecs_ref[2:3, :] = tmp_ref[4:5, :]
    vecs_ref[3:8, :] = jnp.zeros((5, chans), f32)


def front_kernel(xp_ref, wexp, tmp_ref, w1_hbm, b1_hbm, w2_hbm,
                 yn_ref, normed_ref, rstd_ref, mean_ref, w1_ref, b1_ref, w2_ref, sems):
    blocks, rows, padded, _ = xp_ref.shape
    cols = padded - 2 * EDGE
    chans = blocks * LANES
    half = cols // 4
    moves = [(w1_hbm, w1_ref), (b1_hbm, b1_ref), (w2_hbm, w2_ref)]
    copies = [pltpu.make_async_copy(src, dst, sems.at[k]) for k, (src, dst) in enumerate(moves)]
    for copy in copies:
        copy.start()
    mean_ref[...] = jnp.zeros(mean_ref.shape, f32)

    def conv_step(c, carry):
        lanes = pl.ds(pl.multiple_of(c * LANES, LANES), LANES)
        for part in range(4):
            acc = conv_block(xp_ref, c, wexp, rows, part * half, half, False)
            bias = tmp_ref[0:1, lanes]
            for h in range(rows):
                at = slice(h * cols + part * half, h * cols + part * half + half)
                value = acc[h].reshape(half, LANES) + bias
                normed_ref[at, lanes] = value
                mean_ref[at, :] = mean_ref[at, :] + value
        return carry

    lax.fori_loop(0, blocks, conv_step, 0)
    mean_ref[...] = jnp.broadcast_to(jnp.sum(mean_ref[...], axis=-1, keepdims=True) * (1.0 / chans), mean_ref.shape)

    def spread_step(r, carry):
        at = pl.ds(pl.multiple_of(r * cols, cols), cols)
        mean = mean_ref[at, :]
        total = jnp.zeros((cols, LANES), f32)
        for c in range(blocks):
            d = normed_ref[at, c * LANES : (c + 1) * LANES] - mean
            total = total + d * d
        rstd_ref[at, :] = total
        return carry

    lax.fori_loop(0, rows, spread_step, 0)
    var = jnp.sum(rstd_ref[...], axis=-1, keepdims=True) * (1.0 / chans)
    rstd_ref[...] = jnp.broadcast_to(lax.rsqrt(var + 1e-06), rstd_ref.shape)
    gain, shift = tmp_ref[1:2, :], tmp_ref[2:3, :]

    def norm_step(r, carry):
        at = pl.ds(pl.multiple_of(r * cols, cols), cols)
        mean, rs = mean_ref[at, :], rstd_ref[at, :]
        for c in range(blocks):
            lanes = slice(c * LANES, (c + 1) * LANES)
            normed = (normed_ref[at, lanes] - mean) * rs
            yn_ref[at, lanes] = (normed * gain[:, lanes] + shift[:, lanes]).astype(bf16)
        return carry

    lax.fori_loop(0, rows, norm_step, 0)
    for copy in copies:
        copy.wait()


def gate(pre):
    return 0.5 * (1.0 + lax.erf(pre * root_half))


def split_store(core, part, value, keep_ref, send_ref, row):
    for side in range(2):
        @pl.when(core == side)
        def _(side=side):
            k, s = side * part, (1 - side) * part
            keep_ref[row : row + part, :] = value[k : k + part, :]
            send_ref[row : row + part, :] = value[s : s + part, :]


def slope_of(pre, cdf):
    density = jnp.exp(-0.5 * pre * pre) * inv_root_two_pi
    return cdf + pre * density


def open_kernel(yn_ref, w1_ref, b1_ref, rise_ref, keep_ref, send_ref, *, slot):
    wide = rise_ref.shape[1]
    chip, core = place()
    at = pl.multiple_of(slot(chip) * wide, wide)
    pre = dot_last(yn_ref[...], w1_ref[pl.ds(at, wide), :]) + b1_ref[:, pl.ds(at, wide)]
    cdf = gate(pre)
    rise_ref[...] = slope_of(pre, cdf)
    split_store(core, wide // 2, (pre * cdf).astype(bf16).T, keep_ref, send_ref, 0)


def close_kernel(gp_ref, rise_ref, w2_ref, gpre_ref, keep_ref, send_ref, *, slot):
    wide = rise_ref.shape[1]
    chip, core = place()
    at = pl.multiple_of(slot(chip) * wide, wide)
    gpre = (dot(gp_ref[...], w2_ref[:, pl.ds(at, wide)]) * rise_ref[...]).astype(bf16)
    gpre_ref[...] = gpre
    split_store(core, wide // 2, gpre.T, keep_ref, send_ref, 0)


def wide_kernel(yn_ref, gp_ref, w1_ref, b1_ref, w2_ref, *rest, mode, slot, other):
    *more, bsum_ref, keep_ref, send_ref = rest
    wide = bsum_ref.shape[1]
    part = wide // 2
    chip, core = place()
    at = pl.multiple_of(slot(chip) * wide, wide)
    w1 = w1_ref[pl.ds(at, wide), :]
    w2 = w2_ref[:, pl.ds(at, wide)]
    pre = dot_last(yn_ref[...], w1) + b1_ref[:, pl.ds(at, wide)]
    cdf = gate(pre)
    hidden = (pre * cdf).astype(bf16)
    gpre = (dot(gp_ref[...], w2) * slope_of(pre, cdf)).astype(bf16)
    bsum_ref[...] = jnp.broadcast_to(jnp.sum(gpre.astype(f32), axis=0, keepdims=True), (8, wide))
    gn = dot(gpre, w1)
    if mode == "first":
        (gn_ref,) = more
        gn_ref[...] = gn
    elif mode == "next":
        gin_ref, gn_ref = more
        gn_ref[...] = gin_ref[...] + gn
    else:
        gpre_ref, gn_ref, osum_ref = more
        back = pl.multiple_of(other(chip) * wide, wide)
        gn_ref[...] = gn + dot(gpre_ref[...], w1_ref[pl.ds(back, wide), :])
        total = jnp.sum(gpre_ref[...].astype(f32), axis=0, keepdims=True)
        osum_ref[...] = jnp.broadcast_to(total, (8, wide))
    split_store(core, part, gpre.T, keep_ref, send_ref, 0)
    split_store(core, part, hidden.T, keep_ref, send_ref, part)


def half_kernel(own_ref, sib_ref, keep_ref, got_ref, *rest, slot):
    if slot is None:
        (d_ref,) = rest
    else:
        w2_ref, d_ref, scale_ref = rest
    d = dot(keep_ref[...], own_ref[...]) + dot(got_ref[...], sib_ref[...])
    d_ref[...] = d.astype(d_ref.dtype)
    if slot is not None:
        part, chans = d.shape
        chip, core = place()
        at = pl.multiple_of((2 * slot(chip) + core) * part, part)
        prod = d * w2_ref[:, pl.ds(at, part)].T.astype(f32)
        scale_ref[...] = jnp.sum(prod.reshape(part // 8, 8, chans), axis=0)


def share_kernel(w2_ref, yo_ref, ys_ref, go_ref, gs_ref, keep_ref, got_ref, d1_ref, d2_ref, scale_ref, *, slot):
    part = keep_ref.shape[0] // 2
    first, second = slice(0, part), slice(part, 2 * part)
    half_kernel(yo_ref, ys_ref, keep_ref.at[first, :], got_ref.at[first, :], d1_ref, slot=None)
    half_kernel(go_ref, gs_ref, keep_ref.at[second, :], got_ref.at[second, :], w2_ref, d2_ref, scale_ref, slot=slot)


def relay_kernel(direct_ref, base_ref, more_ref, pack_ref):
    part = direct_ref.shape[0]
    pack_ref[0:part, :] = direct_ref[...]
    pack_ref[part:, :] = (base_ref[...] + more_ref[...].astype(f32)).astype(bf16)


def slope_kernel(gn_ref, raw_ref, mean_ref, rstd_ref, vecs_ref, gp_ref, g_ref, gd_ref, sums_ref):
    blocks, rows, padded, _ = gd_ref.shape
    cols = padded - 2 * EDGE
    chans = blocks * LANES
    zero_edges(gd_ref, blocks, rows, cols)
    gain = vecs_ref[0:1, :]

    def norm_step(r, carry):
        at = pl.ds(pl.multiple_of(r * cols, cols), cols)
        gn = gn_ref[at, :]
        rs = rstd_ref[at, 0:1]
        normed = (raw_ref[at, :] - mean_ref[at, 0:1]) * rs
        prod = gn * normed
        scaled = gn * gain
        mean_a = jnp.mean(scaled, axis=-1, keepdims=True)
        mean_b = jnp.mean(prod * gain, axis=-1, keepdims=True)
        gd = rs * (scaled - mean_a - normed * mean_b)
        for c in range(blocks):
            gd_ref[c, r, EDGE : EDGE + cols, :] = gd[:, c * LANES : (c + 1) * LANES]
        fold = lambda v: jnp.sum(v.reshape(cols // 8, 8, chans), axis=0)
        parts = (gd, prod, gn, gp_ref[at, :].astype(f32), g_ref[r].astype(f32))
        return tuple(old + fold(part) for old, part in zip(carry, parts))

    zero = jnp.zeros((8, chans), f32)
    sums = lax.fori_loop(0, rows, norm_step, (zero,) * 5)
    for k in range(5):
        sums_ref[k : k + 1, :] = jnp.sum(sums[k], axis=0, keepdims=True)
    sums_ref[5:8, :] = jnp.zeros((3, chans), f32)


def back_kernel(gd_ref, g_ref, wexp, gi_ref):
    rows, cols, chans = g_ref.shape
    blocks = chans // LANES
    half = cols // 4

    def conv_step(c, carry):
        lanes = pl.ds(pl.multiple_of(c * LANES, LANES), LANES)
        for part in range(4):
            acc = conv_block(gd_ref, c, wexp, rows, part * half, half, True)
            for h in range(rows):
                span = slice(part * half, part * half + half)
                gi_ref[h, span, lanes] = (g_ref[h, span, lanes].astype(f32) + acc[h].reshape(half, LANES)).astype(bf16)
        return carry

    lax.fori_loop(0, blocks, conv_step, 0)


def tap_kernel(xp_ref, gd_ref, vecs_ref, sums_ref, *rest, taps, fast):
    *more, small_ref = rest
    blocks, rows, padded, _ = xp_ref.shape
    cols = padded - 2 * EDGE
    chans = blocks * LANES

    def step(c, carry):
        lanes = pl.ds(pl.multiple_of(c * LANES, LANES), LANES)
        for j in range(7):
            acc = [None] * 7
            for b in range(0, cols, 16):
                grads = [gd_ref[c, h, EDGE + b : EDGE + b + 16, :].reshape(2, 8, LANES) for h in range(rows)]
                for hp in range(rows):
                    at = EDGE + b + j - 3
                    piece = xp_ref[c, hp, at : at + 16, :].reshape(2, 8, LANES)
                    for h in range(max(0, hp - 3), min(rows, hp + 4)):
                        i = hp - h + 3
                        term = grads[h] * piece
                        term = term[0] + term[1]
                        acc[i] = term if acc[i] is None else acc[i] + term
            for i in range(7):
                small_ref[7 * i + j : 7 * i + j + 1, lanes] = jnp.sum(acc[i], axis=0, keepdims=True)
        return carry

    small_ref[taps:, :] = jnp.zeros((small_ref.shape[0] - taps, chans), f32)
    lax.fori_loop(0, blocks, step, 0)
    small_ref[taps : taps + 3, :] = sums_ref[0:3, :]
    small_ref[taps + 3 : taps + 4, :] = sums_ref[3:4, :]
    if fast:
        scales, bsums = more[:4], more[4:]
        total = scales[0][...] + scales[1][...] + scales[2][...] + scales[3][...]
        row = jnp.sum(total, axis=0, keepdims=True) / vecs_ref[1:2, :] + vecs_ref[2:3, :] * sums_ref[4:5, :]
        small_ref[taps + 4 : taps + 5, :] = row
        chip, _ = place()
        for k in range(4):
            small_ref[pl.ds(taps + 5 + lax.bitwise_xor(chip, k), 1), :] = bsums[k][0:1, :]


def merge_kernel(o1_ref, o2_ref, x_ref, y_ref, out1_ref, out2_ref, *, factor):
    part = o1_ref.shape[0]
    out1_ref[...] = (o1_ref[...] + x_ref[0:part, :].astype(f32) + y_ref[part:, :].astype(f32)) * factor
    out2_ref[...] = ((o2_ref[...] + x_ref[part:, :].astype(f32) + y_ref[0:part, :].astype(f32)) * factor).T


def pair_kernel(own_ref, got_ref, total_ref, sent_ref):
    total = own_ref[...] + got_ref[...]
    total_ref[...] = total
    sent_ref[...] = total.astype(bf16)


def gather_kernel(total_ref, near_ref, far_ref, some_ref):
    _, core = place()
    some_ref[...] = near_ref[...].astype(f32)

    @pl.when(core == 0)
    def _():
        some_ref[...] = some_ref[...] + total_ref[...] + far_ref[...].astype(f32)


def emit_kernel(gi_ref, recv_hbm, sem):
    move = pltpu.make_async_copy(gi_ref, recv_hbm, sem)
    move.start()
    move.wait()


def small_kernel(own_ref, got_ref, bias_ref, small_ref, stage_ref, *, factor):
    chans = own_ref.shape[1]
    rows = small_ref.shape[0]
    stage_ref[...] = (own_ref[...] + got_ref[...]) * factor
    for k in range(rows):
        small_ref[k] = stage_ref[k : k + 1, :]
    for k in range(bias_ref.shape[1] // chans):
        bias_ref[:, k * chans : (k + 1) * chans] = stage_ref[rows + k : rows + k + 1, :]


def shifted(block, axis, distance):
    devices = range(lax.axis_size(axis))
    route = [(i - distance, i) for i in devices if i - distance in devices]
    return lax.ppermute(block, axis, route)


def swap(value, bit, count):
    return lax.ppermute(value, "dp", [(i, i ^ bit) for i in range(count)])


def shards(
    block_input,
    grad_output,
    depth_weight,
    depth_bias,
    norm_gain,
    norm_shift,
    pw1_weight,
    pw1_bias,
    pw2_weight,
    pw2_bias,
    layer_scale,
):
    x, g = block_input[0, 0], grad_output[0, 0]
    rows, cols, chans = x.shape
    cells = rows * cols
    blocks = chans // LANES
    taps = depth_weight.shape[1]
    w1, w2 = pw1_weight[0], pw2_weight[0]
    units = w1.shape[0]
    replicas = lax.axis_size("dp")
    factor = 1.0 / replicas
    wide = 768
    part = wide // 2
    fast = replicas == 8 and units == 4 * wide

    wexp = struct((blocks, taps + 42, 8, LANES), f32)
    padded = struct((blocks, rows, cols + 2 * EDGE, LANES), f32)
    like = lambda v: struct(v.shape, v.dtype)
    hbm = pl.BlockSpec(memory_space=pltpu.HBM)
    pin = lambda *vs: tuple(pltpu.with_memory_space_constraint(v, pltpu.HBM) for v in vs)
    vmem = pl.BlockSpec(memory_space=pltpu.VMEM)
    gp, xp, vecs, wexp, gv, tmp = call(
        load_kernel,
        (struct((cells, chans), bf16), padded, struct((8, chans), f32), wexp, like(g), struct((8, chans), f32)),
        *pin(x, g, depth_weight[0], depth_bias, norm_gain, norm_shift, layer_scale, pw2_bias),
        name="load", in_specs=[hbm] * 8, cost=estimate(1e10, 1e6),
        scratch=[pltpu.VMEM(x.shape, bf16), pltpu.VMEM((taps, chans), bf16), pltpu.SemaphoreType.DMA((8,))],
    )
    yn, normed, rstd, mean, w1, b1, w2 = call(
        front_kernel,
        (struct((cells, chans), bf16), struct((cells, chans), f32), struct((cells, LANES), f32),
         struct((cells, LANES), f32), like(w1), like(pw1_bias), like(w2)),
        xp, wexp, tmp, *pin(w1, pw1_bias, w2),
        name="front", in_specs=[vmem] * 3 + [hbm] * 3, cost=estimate(1e10, 1e6),
        scratch=[pltpu.SemaphoreType.DMA((3,))],
    )

    def wide_step(slot, mode, *more, other=None):
        sums = struct((8, wide), f32)
        outs = (struct((cells, chans), f32),) + ((sums,) if mode == "join" else ()) + (
            sums, struct((wide, cells), bf16), struct((wide, cells), bf16))
        return call(
            lambda *refs: wide_kernel(*refs, mode=mode, slot=slot, other=other), outs, yn, gp, w1, b1, w2, *more,
            name="wide", aliases={5: 0} if mode == "next" else {}, cost=estimate(1e10, 1e6),
        )

    def flip(k):
        return lambda chip: lax.bitwise_xor(chip, k)

    def slope(gn):
        return call(slope_kernel, (padded, struct((8, chans), f32)), gn, normed, mean, rstd, vecs, gp, gv,
                    name="slope", cost=estimate(1e6, 1e3))

    if fast:
        gp_s, yn_s = swap(gp, 1, replicas), swap(yn, 1, replicas)
        part_rows = struct((part, cells), bf16)

        def share(k, keep, got, types):
            outs = (struct((part, chans), types[0]), struct((part, chans), types[1]), struct((8, chans), f32))
            return call(lambda *refs: share_kernel(*refs, slot=flip(k)), outs,
                        w2, yn, yn_s, gp, gp_s, keep, got, name="share", cost=estimate(1e6, 1e3))

        rise, keep_h, send_h = call(
            lambda *refs: open_kernel(*refs, slot=flip(3)), (struct((cells, wide), f32), part_rows, part_rows),
            yn, w1, b1, name="open", cost=estimate(1e6, 1e3))
        got_h = swap(send_h, 1, replicas)
        gpre, keep_g, send_g = call(
            lambda *refs: close_kernel(*refs, slot=flip(3)), (struct((cells, wide), bf16), part_rows, part_rows),
            gp, rise, w2, name="close", cost=estimate(1e6, 1e3))
        got_g = swap(send_g, 1, replicas)
        grad = struct((part, chans), bf16)
        gpre, got_h = lax.optimization_barrier((gpre, got_h))
        d2, sc_d = call(lambda *refs: half_kernel(*refs, slot=flip(3)), (grad, struct((8, chans), f32)),
                        gp, gp_s, keep_h, got_h, w2, name="half", cost=estimate(1e6, 1e3))
        d2, got_g = lax.optimization_barrier((d2, got_g))
        d1 = call(lambda *refs: half_kernel(*refs, slot=None), (grad,), yn, yn_s, keep_g, got_g,
                  name="half", cost=estimate(1e6, 1e3))[0]
        gpre, d1 = lax.optimization_barrier((gpre, d1))
        d1_in, d2_in = swap(d1, 2, replicas), swap(d2, 4, replicas)
        gn, bd, bx, keep_x, send_x = wide_step(flip(1), "join", gpre, other=flip(3))
        got_x = swap(send_x, 1, replicas)
        gn, by, keep_y, send_y = wide_step(flip(2), "next", gn)
        got_y = swap(send_y, 1, replicas)
        gn, bo, keep_o, send_o = wide_step(flip(0), "next", gn)
        got_o = swap(send_o, 1, replicas)
        gn, got_x = lax.optimization_barrier((gn, got_x))
        x1, x2, sc_x = share(1, keep_x, got_x, (bf16, f32))
        x1, got_y = lax.optimization_barrier((x1, got_y))
        y1, y2, sc_y = share(2, keep_y, got_y, (f32, bf16))
        y1, gn = lax.optimization_barrier((y1, gn))
        gd, sums = slope(gn)
        gd, x1, x2, y1, y2, d1_in, d2_in = lax.optimization_barrier((gd, x1, x2, y1, y2, d1_in, d2_in))

        def relay(direct, base, more):
            return call(relay_kernel, struct((wide, chans), bf16), direct, base, more,
                        name="relay", cost=estimate(1e6, 1e3))

        pack_x = relay(x1, x2, d2_in)
        y2, pack_x = lax.optimization_barrier((y2, pack_x))
        pack_y = relay(y2, y1, d1_in)
        gd, pack_y = lax.optimization_barrier((gd, pack_y))
        x_in, y_in = swap(pack_x, 2, replicas), swap(pack_y, 4, replicas)
    else:
        core = lax.axis_index("dp") % 2
        gn, bsums, g1, g2 = None, [], [], []
        for p in range(units // wide):
            gn, bsum, keep, send = wide_step(lambda chip, p=p: jnp.int32(p), *(("next", gn) if p else ("first",)))
            lo, hi = jnp.where(core == 0, keep, send), jnp.where(core == 0, send, keep)
            bsums.append(bsum[0:1])
            g1 += [dot(v[:part], yn) for v in (lo, hi)]
            g2 += [dot(v[part:], gp) for v in (lo, hi)]
        g1, g2 = jnp.concatenate(g1, axis=0), jnp.concatenate(g2, axis=0).T

    if not fast:
        gd, sums = slope(gn)
    gi = call(back_kernel, struct((rows, cols, chans), bf16), gd, gv, wexp, name="back", cost=estimate(1e6, 1e3))
    received = shifted(gi, "section", -1)

    if fast:
        o1, o2, sc_o = share(0, keep_o, got_o, (f32, f32))
        more = (sc_d, sc_x, sc_y, sc_o, bo, bx, by, bd)
    else:
        more = ()
    total_rows = -(-(taps + 5 + units // chans) // 8) * 8
    small = call(lambda *refs: tap_kernel(*refs, taps=taps, fast=fast), struct((total_rows, chans), f32),
                 xp, gd, vecs, sums, *more, name="taps", cost=estimate(1e6, 1e3))

    if fast:
        rows_all = struct(small.shape, f32)
        total, sent = call(pair_kernel, (rows_all, struct(small.shape, bf16)), small, swap(small, 1, replicas),
                           name="pair", cost=estimate(1e6, 1e3))
        near = lax.ppermute(sent, "dp", [(i, i ^ (4 if i % 2 else 2)) for i in range(replicas)])
        far = lax.ppermute(sent, "dp", [(i, i ^ 6) for i in range(0, replicas, 2)])
        out1, out2 = call(
            lambda *refs: merge_kernel(*refs, factor=factor),
            (struct((part, chans), f32), struct((chans, part), f32)),
            o1, o2, x_in, y_in, name="merge", cost=estimate(1e6, 1e3))
        out1, total = lax.optimization_barrier((out1, total))
        some = call(gather_kernel, rows_all, total, near, far, name="gather", cost=estimate(1e6, 1e3))
        some_in = swap(some, 1, replicas)
        some, received = lax.optimization_barrier((some, received))
        received = pl.pallas_call(
            emit_kernel, out_shape=like(gi), in_specs=[vmem], out_specs=hbm,
            scratch_shapes=[pltpu.SemaphoreType.DMA],
            compiler_params=pltpu.CompilerParams(vmem_limit_bytes=VMEM_LIMIT), name="emit",
        )(received)
        some, received = lax.optimization_barrier((some, received))
        bias, small = call(
            lambda *refs: small_kernel(*refs, factor=factor),
            (struct((1, units), f32), struct((taps + 5, 1, chans), f32)), some, some_in,
            name="small", scratch=[pltpu.VMEM(small.shape, f32)], cost=estimate(1e6, 1e3))
        small = jnp.transpose(small, (1, 0, 2))
    else:
        scale_sum = jnp.sum(g2 * w2.astype(f32), axis=1)
        gscale = scale_sum / layer_scale[0] + pw2_bias[0] * sums[4]
        small = jnp.concatenate([small[: taps + 4], gscale[None], *bsums], axis=0)
        small = lax.psum(small, "dp")
        out1 = lax.psum_scatter(g1, "dp", scatter_dimension=0, tiled=True) * factor
        out2 = lax.psum_scatter(g2, "dp", scatter_dimension=1, tiled=True) * factor
        small = small * factor
        bias, small = small[taps + 5 :].reshape(1, -1), small[None, : taps + 5]
    return (out1[None], out2[None], bias, small, received[None, None])


def solution(mesh):
    in_specs = (
        P("section", "dp", None, None, None),
        P("section", "dp", None, None, None),
        P("section", None, None),
        P("section", None),
        P("section", None),
        P("section", None),
        P("section", None, None),
        P("section", None),
        P("section", None, None),
        P("section", None),
        P("section", None),
    )
    out_specs = (
        P("section", "dp", None),
        P("section", None, "dp"),
        P("section", None),
        P("section", None, None),
        P("section", "dp", None, None, None),
    )
    return jax.shard_map(shards, mesh=mesh, in_specs=in_specs, out_specs=out_specs, check_vma=False)
```
